128 devices in a mesh: row: 8 (over y, core), col: 16 (over z, x).
Axes of the slice: x: 4, y: 4, z: 4, core: 2. Of those that a mesh axis runs over, the one named last changes fastest.
Arguments:
- child_fronts: float32 [2, 8192, 8192], P(None, 'row', 'col'), as said below
- parent_front: float32 [12288, 12288], P('row', 'col'), as said below
- child_map: int32 [2, 7168], replicated, may hold values from 0 to 12287, as said below
Outputs:
- child_factor: float32 [2, 8192, 1024], P(None, 'row', 'col')
- parent_factor: float32 [12288, 256], P('row', 'col')
- parent_schur: float32 [12288, 12288], P('row', 'col')
The draws below stay inside these ranges and needn't reach their ends.
Inputs may be any that keep to these rules, and one draw needn't show every extreme that they name: child_fronts[k] and parent_front are symmetric positive definite. parent_front is symmetric positive definite. The entries of child_map[k] are distinct. Each aligned block of 512 entries of child_map[k] names exactly 32 indices in each aligned block of 768 parent indices.
All inputs are finite; a program needn't handle non-finite values.
Results may differ from the reference program's by a relative error of at most 0.0003.
Values sent between devices are 32-bit elements; how exact they have to be, the bound alone decides.
No kernel may reach another device: no remote copies, remote signals or barrier semaphores. Data moves between devices by JAX's collectives and lax.ppermute only.
A program may use at most 192 MiB of HBM per device.

```python
import jax
import jax.numpy as jnp
from jax import lax

WC = 8192
WP = 12288
PC = 1024
PP = 256
NB = 256
NS = 7168
CCOLS = 512
PCOLS = 768
QCOL = 32
N_COL = 16


def spd_matrix(key, width):
    base_key = jax.random.fold_in(key, 0)
    shift_key = jax.random.fold_in(key, 1)
    vector_key = jax.random.fold_in(key, 3)
    base = jax.random.normal(base_key, (width, width), jnp.float32)
    gram = jnp.dot(base, base.T, precision=lax.Precision.HIGHEST)
    shift = jax.random.uniform(shift_key, (width,), jnp.float32, 0.25, 1.0) * width
    direction = jax.random.normal(vector_key, (width,), jnp.float32)
    coupling = 0.5 * width * (direction[:, None] * direction[None, :])
    matrix = (gram + jnp.diag(shift) + coupling) / jnp.sqrt(jnp.float32(width))
    matrix = 0.5 * (matrix + matrix.T)
    return matrix


def draw_child_fronts(key, part):
    return jnp.stack([spd_matrix(jax.random.fold_in(key, 11 + which), WC) for which in range(2)], axis=0)


def draw_parent_front(key, part):
    return spd_matrix(jax.random.fold_in(key, 29), WP)


def one_map(key):
    source_blocks = NS // CCOLS
    dest_key, place_key = jax.random.split(key)
    dest_keys = jax.random.split(dest_key, N_COL)
    offsets = jax.vmap(lambda single: jax.random.permutation(single, PCOLS))(dest_keys)
    offsets = offsets[:, :source_blocks * QCOL].reshape(N_COL, source_blocks, QCOL)
    bases = (jnp.arange(N_COL, dtype=jnp.int32) * PCOLS)[:, None, None]
    values = jnp.transpose(offsets.astype(jnp.int32) + bases, (1, 0, 2)).reshape(source_blocks, CCOLS)
    place_keys = jax.random.split(place_key, source_blocks)
    places = jax.vmap(lambda single: jax.random.permutation(single, CCOLS))(place_keys)
    inverse = jnp.argsort(places, axis=1)
    mapped = jnp.take_along_axis(values, inverse, axis=1)
    return mapped.reshape(NS).astype(jnp.int32)


def draw_child_map(key, part):
    return jnp.stack([one_map(jax.random.fold_in(key, 47 + which)) for which in range(2)], axis=0)


def setup_inputs(seed: int = 0) -> dict:
    seeds = jax.random.split(jax.random.key(seed), 4)
    return {
        "child_fronts": draw_child_fronts(jax.random.fold_in(seeds[3], 71), 0),
        "parent_front": draw_parent_front(jax.random.fold_in(seeds[3], 71), 0),
        "child_map": draw_child_map(jax.random.fold_in(seeds[3], 71), 0),
    }


def eliminate_panels(front, pivots):
    width = front.shape[0]
    panels = []
    for panel_step in range(pivots // NB):
        offset = panel_step * NB
        corner = front[offset:offset + NB, offset:offset + NB]
        factor = jnp.linalg.cholesky(corner)
        below = front[offset:, offset:offset + NB]
        solved = jax.scipy.linalg.solve_triangular(factor, below.T, lower=True).T
        update = jnp.dot(solved, solved.T, precision=lax.Precision.HIGHEST)
        front = front.at[offset:, offset:].add(-update)
        panels.append(jnp.concatenate([jnp.zeros((offset, NB), jnp.float32), solved], axis=0))
    return (front, jnp.concatenate(panels, axis=1))

def reference(child_fronts, parent_front, child_map):
    merged = parent_front
    factors = []
    for which_child in range(2):
        updated, panels = eliminate_panels(child_fronts[which_child], PC)
        factors.append(panels)
        schur = updated[PC:, PC:]
        targets = child_map[which_child]
        merged = merged.at[targets[:, None], targets[None, :]].add(schur)
    child_factor = jnp.stack(factors, axis=0)
    updated, parent_factor = eliminate_panels(merged, PP)
    index = jnp.arange(WP, dtype=jnp.int32)
    keep = (index[:, None] >= PP) & (index[None, :] >= PP)
    parent_schur = jnp.where(keep, updated, jnp.float32(0.0))
    return (child_factor, parent_factor, parent_schur)
```

```python
from functools import partial

import jax
import jax.numpy as jnp
from jax import lax
from jax.experimental import pallas as pl
from jax.experimental.pallas import tpu as pltpu
from jax.sharding import PartitionSpec as P

F32 = jnp.float32
BF16 = jnp.bfloat16
NB = 256
SB = 64
GROUP = 4
BLK = 512
KEYS = 16
HIGHEST = lax.Precision.HIGHEST
VMEM_LIMIT = 56 << 20


def mm(a, b, ca, cb):
    return lax.dot_general(
        a, b, (((ca,), (cb,)), ((), ())), precision=HIGHEST, preferred_element_type=F32
    )


def mm_bf(a, b, ca, cb):
    return lax.dot_general(a, b, (((ca,), (cb,)), ((), ())), preferred_element_type=F32)


def split3(x):
    hi = x.astype(BF16)
    rest = x - hi.astype(F32)
    mid = rest.astype(BF16)
    low = (rest - mid.astype(F32)).astype(BF16)
    return hi, mid, low


def call(kernel, name, **kw):
    return pl.pallas_call(
        kernel,
        name=name,
        compiler_params=pltpu.CompilerParams(vmem_limit_bytes=VMEM_LIMIT),
        **kw,
    )


def factor_small(diag):
    n = SB
    ri = lax.broadcasted_iota(jnp.int32, (n, n), 0)
    ci = lax.broadcasted_iota(jnp.int32, (n, n), 1)
    full = jnp.concatenate([diag, jnp.where(ri == ci, 1.0, 0.0)], axis=1)
    nv = n // 8
    rows = [full[8 * v : 8 * v + 8, :] for v in range(nv)]
    sub = lax.broadcasted_iota(jnp.int32, (8, 2 * n), 0)
    wide = lambda x: jnp.broadcast_to(x, (8, 2 * n))
    pivots = []
    for j0 in range(0, n, GROUP):
        v0 = j0 // 8
        cols = [[wide(rows[v][:, j0 + q : j0 + q + 1]) for v in range(v0, nv)] for q in range(GROUP)]
        at = [(j0 + q) % 8 for q in range(GROUP)]
        lead = [wide(rows[v0][at[q] : at[q] + 1, :]) for q in range(GROUP)]
        for q in range(GROUP):
            inv = 1.0 / wide(cols[q][0][at[q] : at[q] + 1, :])
            pivots.append(inv)
            scaled = lead[q] * inv
            below = [jnp.where(sub > at[q], cols[q][0], 0.0)] + cols[q][1:]
            for t in range(q + 1, GROUP):
                ratio = wide(cols[t][0][at[q] : at[q] + 1, :]) * inv
                weight = wide(cols[q][0][at[t] : at[t] + 1, :])
                cols[t] = [cols[t][i] - below[i] * ratio for i in range(len(below))]
                lead[t] = lead[t] - weight * scaled
            for i in range(len(below)):
                rows[v0 + i] = rows[v0 + i] - below[i] * scaled
    out = []
    for v in range(nv):
        scale = pivots[8 * v]
        for s in range(1, 8):
            scale = jnp.where(sub == s, pivots[8 * v + s], scale)
        out.append(rows[v] * jnp.sqrt(scale))
    return jnp.concatenate(out, axis=0)


def factor_diag(d_ref, w_ref, base):
    ri = lax.broadcasted_iota(jnp.int32, (NB, NB), 0)
    ci = lax.broadcasted_iota(jnp.int32, (NB, NB), 1)
    w_ref[...] = jnp.where(ri == ci, 1.0, 0.0)
    cb = lax.broadcasted_iota(jnp.int32, (SB, NB), 1)
    rb = lax.broadcasted_iota(jnp.int32, (SB, NB), 0)
    for lo in range(0, NB, SB):
        hi = lo + SB
        strip = d_ref[base + lo : base + hi, base : base + NB]
        small = factor_small(strip[:, lo:hi])
        both = mm(small[:, SB:], jnp.concatenate([strip, w_ref[lo:hi, :]], axis=1), 1, 0)
        up = jnp.where(cb >= rb + lo, both[:, :NB], 0.0)
        inv = jnp.where(cb <= rb + lo, both[:, NB:], 0.0)
        d_ref[base + lo : base + hi, base : base + NB] = up
        w_ref[lo:hi, :] = inv
        if hi < NB:
            update = mm(up[:, hi:], jnp.concatenate([up, inv], axis=1), 0, 0)
            d_ref[base + hi : base + NB, base : base + NB] -= update[:, :NB]
            w_ref[hi:, :] -= update[:, NB:]


def factor_all(n, u_ref, w_ref):
    for lo in range(0, n, NB):
        hi = lo + NB
        factor_diag(u_ref, w_ref.at[lo // NB], lo)
        if hi < n:
            right = mm(w_ref[lo // NB], u_ref[lo:hi, hi:], 1, 0)
            u_ref[lo:hi, hi:] = right
            u_ref[hi:, hi:] -= mm(right, right, 0, 0)
    for lo in range(NB, n, NB):
        u_ref[lo : lo + NB, :lo] = jnp.zeros((NB, lo), F32)


def chol_kernel(n, a_ref, u_ref, w_ref):
    u_ref[...] = a_ref[...]
    factor_all(n, u_ref, w_ref)


def cholesky_upper(a, name):
    n = a.shape[0]
    return call(
        partial(chol_kernel, n),
        name,
        out_shape=(
            jax.ShapeDtypeStruct((n, n), F32),
            jax.ShapeDtypeStruct((n // NB, NB, NB), F32),
        ),
    )(a)


def one_hot(pos_row, n):
    ids = lax.broadcasted_iota(jnp.int32, (n, pos_row.shape[1]), 0)
    return jnp.where(ids == pos_row, 1.0, 0.0).astype(BF16)


def pack_x_kernel(flag_ref, pos_ref, f_ref, o_ref):
    pivot = flag_ref[0] != 0

    @pl.when(pivot)
    def _():
        for y in range(4):
            for q in range(4):
                o_ref[y, 0, q * NB : (q + 1) * NB, :] = f_ref[
                    0, y * NB : (y + 1) * NB, q * 128 : (q + 1) * 128
                ]

    @pl.when(jnp.logical_not(pivot))
    def _():
        place = one_hot(pos_ref[0], BLK)
        out = sum(mm_bf(part, place, 1, 1) for part in split3(f_ref[0]))
        for y in range(4):
            o_ref[y, 0] = out[:, y * 128 : (y + 1) * 128]


def pack_kernel(flag_ref, pos_ref, f_ref, o_ref):
    pivot = flag_ref[0] != 0
    for b in range(2):
        place_row = one_hot(pos_ref[0, b : b + 1, :], BLK)
        parts = split3(f_ref[0, b * BLK : (b + 1) * BLK, :])
        rows = [mm_bf(place_row, part, 1, 0) for part in parts]

        def store(total):
            for y in range(4):
                for p in range(KEYS):
                    o_ref[y, 0, p, b * 32 : (b + 1) * 32, :] = total[
                        p * 32 : (p + 1) * 32, y * 128 : (y + 1) * 128
                    ]

        @pl.when(pivot)
        def _():
            store(rows[0] + rows[1] + rows[2])

        @pl.when(jnp.logical_not(pivot))
        def _():
            place_col = one_hot(pos_ref[0, 2:3, :], BLK)
            store(sum(mm_bf(place_col, row.astype(BF16), 1, 1) for row in rows))


def chol_gathered_kernel(a_ref, u_ref, w_ref):
    for yy in range(4):
        for pc in range(KEYS):
            q, i = pc // 4, pc % 4
            for h in range(2):
                u_ref[
                    yy * NB + i * 64 : yy * NB + i * 64 + 64,
                    h * BLK + q * 128 : h * BLK + q * 128 + 128,
                ] = a_ref[yy * KEYS + pc, h]
    factor_all(u_ref.shape[0], u_ref, w_ref)


def panel_kernel(u_ref, w_ref, y_ref, x_ref, c_ref, rx_ref, s_ref, ry_ref):
    step = pl.program_id(0)
    panels = u_ref.shape[0] // NB

    @pl.when(step == 0)
    def _():
        for p in range(panels):
            lanes = [(2 * p + t) // 4 for t in range(2)]
            which = [(2 * p + t) % 4 for t in range(2)]
            cur = jnp.concatenate(
                [y_ref[which[t], :, lanes[t]].reshape(448, 128) for t in range(2)], axis=1
            )
            if p:
                cur = cur - mm(ry_ref[:, : p * NB], u_ref[: p * NB, p * NB : (p + 1) * NB], 1, 0)
            ry_ref[:, p * NB : (p + 1) * NB] = mm(cur, w_ref[p], 1, 1)

    for p in range(panels):
        lo, hi = p * NB, (p + 1) * NB
        cur = jnp.concatenate([x_ref[0, lo:hi, :], x_ref[1, lo:hi, :]], axis=1)
        if p:
            cur = cur - mm(u_ref[:lo, lo:hi], rx_ref[:lo, :], 0, 0)
        rx_ref[lo:hi, :] = mm(w_ref[p], cur, 1, 0)
    prod = mm(ry_ref[...], rx_ref[...], 1, 0)
    c0 = c_ref[0, 2:, 0:32, :].reshape(448, 128) - prod[:, :128]
    c1 = c_ref[0, 2:, 32:64, :].reshape(448, 128) - prod[:, 128:]
    lane = lax.broadcasted_iota(jnp.int32, (448, 128), 1)
    s_ref[0] = jnp.where(lane < 64, c0, pltpu.roll(c1, 64, 1))
    s_ref[1] = jnp.where(lane < 64, pltpu.roll(c0, 64, 1), c1)


def unpack_kernel(src_ref, r_ref, o_ref):
    for k in range(2):
        wide = jnp.concatenate([r_ref[2 * yy + k] for yy in range(4)], axis=1)
        place = one_hot_rows(src_ref[k], 1024)
        o_ref[k] = sum(mm_bf(place, part, 1, 1) for part in split3(wide))


def one_hot_rows(src_col, n):
    ids = lax.broadcasted_iota(jnp.int32, (src_col.shape[0], n), 1)
    return jnp.where(ids == src_col, 1.0, 0.0).astype(BF16)


def merge_kernel(tx_ref, ty_ref, s_ref, p_ref, o_ref, part_ref, ey_ref):
    tile = pl.program_id(0)

    @pl.when(tile == 0)
    def _():
        for k in range(2):
            ey_ref[k] = one_hot(ty_ref[k], 768)
            for i, part in enumerate(split3(s_ref[k])):
                part_ref[k, i] = part

    acc = p_ref[...]
    for k in range(2):
        ex = one_hot(tx_ref[k] - tile * NB, NB)
        for i in range(3):
            half = mm_bf(ex, part_ref[k, i], 1, 1)
            acc = acc + mm_bf(half.astype(BF16), ey_ref[k], 1, 1)
    o_ref[...] = acc


def final_kernel(flag_ref, w_ref, m_ref, row_ref, col_ref, o_ref, f_ref, rc_ref):
    tile = pl.program_id(0)

    @pl.when(tile == 0)
    def _():
        rc_ref[...] = mm(w_ref[0], col_ref[...], 1, 0)

    rows = mm(row_ref[...], w_ref[0], 1, 1)
    f_ref[...] = rows
    out = m_ref[...] - mm(rows, rc_ref[...], 1, 0)
    lane = lax.broadcasted_iota(jnp.int32, out.shape, 1)
    keep_row = jnp.logical_or(flag_ref[0] != 0, tile > 0)
    keep = jnp.logical_and(keep_row, jnp.logical_or(flag_ref[1] != 0, lane >= NB))
    o_ref[...] = jnp.where(keep, out, 0.0)


def smem():
    return pl.BlockSpec(memory_space=pltpu.SMEM)


def whole(shape):
    return pl.BlockSpec(shape, lambda *_: (0,) * len(shape))


def local(child_fronts, parent_front, child_map):
    r = lax.axis_index("row")
    c = lax.axis_index("col")
    core = r % 2
    y = r // 2
    nblk = child_map.shape[1] // BLK
    parity = [[(2 * i + k) * KEYS + j for i in range(4) for j in range(KEYS)] for k in range(2)]
    parity_row = [[2 * i + k for i in range(4)] for k in range(2)]

    maps = child_map.reshape(2 * nblk, BLK)
    keys = maps // 768
    hot = (keys[:, :, None] == jnp.arange(KEYS, dtype=jnp.int32)).astype(BF16)
    lower = (jnp.arange(BLK)[:, None] >= jnp.arange(BLK)[None, :]).astype(BF16)
    counts = jnp.einsum("ef,bfk->bek", lower, hot, preferred_element_type=F32)
    rank = jnp.sum(counts * hot.astype(F32), axis=2).astype(jnp.int32) - 1
    pos = (keys * 32 + rank).reshape(2, nblk, BLK)
    maps = maps.reshape(2, nblk, BLK)

    pos_c = lax.dynamic_slice_in_dim(pos, jnp.maximum(c - 2, 0), 1, axis=1)
    pos_r = lax.dynamic_slice_in_dim(pos, jnp.maximum(2 * r - 2, 0), 2, axis=1)
    flag = (c < 2).astype(jnp.int32)[None]

    packed_x = call(
        pack_x_kernel,
        "pack_x",
        grid=(2,),
        in_specs=[
            smem(),
            pl.BlockSpec((1, 1, BLK), lambda k: (k, 0, 0)),
            pl.BlockSpec((1, 1024, BLK), lambda k: (k, 0, 0)),
        ],
        out_specs=pl.BlockSpec((4, 1, 1024, 128), lambda k: (0, k, 0, 0)),
        out_shape=jax.ShapeDtypeStruct((4, 2, 1024, 128), F32),
    )(flag, pos_c, child_fronts)
    own = packed_x[0, 0]
    for dest in range(1, 8):
        got = lax.ppermute(packed_x[dest // 2, dest % 2], "row", [(0, dest)])
        own = jnp.where(r == dest, got, own)

    spread = lax.all_to_all(own.reshape(KEYS, 64, 128), "col", split_axis=0, concat_axis=0, tiled=True)
    pieces = lax.all_gather(spread[:2], ("row", "col"), axis_index_groups=parity)
    upper, inverses = call(
        chol_gathered_kernel,
        "child_factor",
        out_shape=(
            jax.ShapeDtypeStruct((1024, 1024), F32),
            jax.ShapeDtypeStruct((4, NB, NB), F32),
        ),
    )(pieces)
    own, pieces = lax.optimization_barrier((own, spread))
    panel_x = lax.all_gather(own, "col")

    packed = call(
        pack_kernel,
        "pack",
        grid=(2,),
        in_specs=[
            smem(),
            pl.BlockSpec((1, 3, BLK), lambda k: (k, 0, 0)),
            pl.BlockSpec((1, 1024, BLK), lambda k: (k, 0, 0)),
        ],
        out_specs=pl.BlockSpec((4, 1, KEYS, 64, 128), lambda k: (0, k, 0, 0, 0)),
        out_shape=jax.ShapeDtypeStruct((4, 2, KEYS, 64, 128), F32),
    )(flag, jnp.concatenate([pos_r, pos_c], axis=1), child_fronts)
    arrived = lax.all_to_all(
        packed.reshape(8 * KEYS, 64, 128), ("row", "col"), split_axis=0, concat_axis=0, tiled=True
    ).reshape(8, KEYS, 64, 128)
    panel_y = lax.all_gather(arrived[1:, :2], "row", axis_index_groups=parity_row)

    factor_x, schur = call(
        panel_kernel,
        "panel",
        grid=(7,),
        in_specs=[
            whole((1024, 1024)),
            whole((4, NB, NB)),
            whole((4, 7, 2, 64, 128)),
            pl.BlockSpec((pl.Element(2), pl.Element(1024), pl.Element(128)), lambda g: (2 * g + 2, 0, 0)),
            pl.BlockSpec((1, KEYS, 64, 128), lambda g: (g + 1, 0, 0, 0)),
        ],
        out_specs=(
            pl.BlockSpec((1024, NB), lambda g: (0, g)),
            pl.BlockSpec((2, 448, 128), lambda g: (0, 0, g)),
        ),
        out_shape=(
            jax.ShapeDtypeStruct((1024, 1792), F32),
            jax.ShapeDtypeStruct((2, 448, 896), F32),
        ),
        scratch_shapes=[pltpu.VMEM((448, 1024), F32)],
    )(upper, inverses, panel_y, panel_x, arrived)

    mine = lax.dynamic_index_in_dim(schur, core, 0, keepdims=False)
    other = lax.dynamic_index_in_dim(schur, 1 - core, 0, keepdims=False)
    got = lax.ppermute(other, "row", [(i, i ^ 1) for i in range(8)])
    first = core == 0
    both = jnp.stack([jnp.where(first, mine, got), jnp.where(first, got, mine)])

    strip = lax.dynamic_slice_in_dim(factor_x, c * 64, 64, axis=0)
    head = lax.dynamic_slice(upper, (c * 64, y * NB), (64, NB))
    outgoing = jnp.concatenate([head[None], jnp.stack(jnp.split(strip, 7, axis=1))])
    landed = lax.all_to_all(outgoing, "row", split_axis=0, concat_axis=0, tiled=True)
    spot = (pos_r // 128) * NB + jnp.arange(2, dtype=jnp.int32)[None, :, None] * 128 + pos_r % 128
    natural = jnp.broadcast_to(jnp.arange(1024, dtype=jnp.int32), (2, 1024))
    spot = jnp.where(r == 0, natural, spot.reshape(2, 1024))
    child_factor = call(
        unpack_kernel, "unpack", out_shape=jax.ShapeDtypeStruct((2, 1024, 64), F32)
    )(spot[:, :, None], landed)

    def sorted_maps(start, count):
        ids = start + jnp.arange(count, dtype=jnp.int32)
        return jnp.sum(
            jnp.where(pos[:, :, :, None] == ids, maps[:, :, :, None], 0), axis=2, dtype=jnp.int32
        )

    to_rows = sorted_maps(r * 64, 64).reshape(2, 1, 896) - r * 1536
    to_cols = sorted_maps(c * 32, 32).reshape(2, 1, 448) - c * 768
    merged = call(
        merge_kernel,
        "merge",
        grid=(6,),
        in_specs=[
            whole((2, 1, 896)),
            whole((2, 1, 448)),
            whole((2, 448, 896)),
            pl.BlockSpec((NB, 768), lambda t: (t, 0)),
        ],
        out_specs=pl.BlockSpec((NB, 768), lambda t: (t, 0)),
        out_shape=jax.ShapeDtypeStruct((1536, 768), F32),
        scratch_shapes=[pltpu.VMEM((2, 3, 448, 896), BF16), pltpu.VMEM((2, 768, 448), BF16)],
    )(to_rows, to_cols, both, parent_front)

    down = lax.all_to_all(merged[:NB].reshape(8, 32, 768), "row", split_axis=0, concat_axis=0, tiled=True)
    top = lax.all_gather(down[0], "row").reshape(NB, 768)
    side = jnp.concatenate([merged[:, :NB], top[:, :NB]]).reshape(KEYS, 112, NB)
    across = lax.all_to_all(side, "col", split_axis=0, concat_axis=0, tiled=True)
    left = lax.all_gather(across[0], "col").reshape(1792, NB)
    _, parent_inverse = cholesky_upper(left[1536:], "parent_factor")
    schur_out, rows_out = call(
        final_kernel,
        "final",
        grid=(6,),
        in_specs=[
            smem(),
            whole((1, NB, NB)),
            pl.BlockSpec((NB, 768), lambda t: (t, 0)),
            pl.BlockSpec((NB, NB), lambda t: (t, 0)),
            whole((NB, 768)),
        ],
        out_specs=(
            pl.BlockSpec((NB, 768), lambda t: (t, 0)),
            pl.BlockSpec((NB, NB), lambda t: (t, 0)),
        ),
        out_shape=(
            jax.ShapeDtypeStruct((1536, 768), F32),
            jax.ShapeDtypeStruct((1536, NB), F32),
        ),
        scratch_shapes=[pltpu.VMEM((NB, 768), F32)],
    )(jnp.stack([r, c]), parent_inverse, merged, left, top)
    parent_factor = lax.dynamic_slice_in_dim(rows_out, c * 16, 16, axis=1)
    return child_factor, parent_factor, schur_out


def solution(mesh):
    return jax.shard_map(
        local,
        mesh=mesh,
        in_specs=(P(None, "row", "col"), P("row", "col"), P()),
        out_specs=(P(None, "row", "col"), P("row", "col"), P("row", "col")),
        check_vma=False,
    )
```

```python
from functools import partial

import jax
import jax.numpy as jnp
from jax import lax
from jax.experimental import pallas as pl
from jax.experimental.pallas import tpu as pltpu
from jax.sharding import PartitionSpec as P

F32 = jnp.float32
BF16 = jnp.bfloat16
NB = 256
SB = 64
GROUP = 4
BLK = 512
KEYS = 16
HIGHEST = lax.Precision.HIGHEST
VMEM_LIMIT = 56 << 20


def mm(a, b, ca, cb):
    return lax.dot_general(
        a, b, (((ca,), (cb,)), ((), ())), precision=HIGHEST, preferred_element_type=F32
    )


def mm_bf(a, b, ca, cb):
    return lax.dot_general(a, b, (((ca,), (cb,)), ((), ())), preferred_element_type=F32)


def split2(x):
    hi = x.astype(BF16)
    return hi, (x - hi.astype(F32)).astype(BF16)


def mm3(a, b, ca, cb):
    return mm_bf(a[0], b[0], ca, cb) + (mm_bf(a[0], b[1], ca, cb) + mm_bf(a[1], b[0], ca, cb))


def split3(x):
    hi = x.astype(BF16)
    rest = x - hi.astype(F32)
    mid = rest.astype(BF16)
    low = (rest - mid.astype(F32)).astype(BF16)
    return hi, mid, low


def call(kernel, name, us, **kw):
    return pl.pallas_call(
        kernel,
        name=name,
        cost_estimate=pl.CostEstimate(flops=us * 10**9, transcendentals=0, bytes_accessed=1 << 20),
        compiler_params=pltpu.CompilerParams(vmem_limit_bytes=VMEM_LIMIT),
        **kw,
    )


def factor_small(diag):
    n = SB
    ri = lax.broadcasted_iota(jnp.int32, (n, n), 0)
    ci = lax.broadcasted_iota(jnp.int32, (n, n), 1)
    full = jnp.concatenate([diag, jnp.where(ri == ci, 1.0, 0.0)], axis=1)
    nv = n // 8
    rows = [full[8 * v : 8 * v + 8, :] for v in range(nv)]
    sub = lax.broadcasted_iota(jnp.int32, (8, 2 * n), 0)
    wide = lambda x: jnp.broadcast_to(x, (8, 2 * n))
    pivots = []
    for j0 in range(0, n, GROUP):
        v0 = j0 // 8
        cols = [[wide(rows[v][:, j0 + q : j0 + q + 1]) for v in range(v0, nv)] for q in range(GROUP)]
        at = [(j0 + q) % 8 for q in range(GROUP)]
        lead = [wide(rows[v0][at[q] : at[q] + 1, :]) for q in range(GROUP)]
        for q in range(GROUP):
            inv = 1.0 / wide(cols[q][0][at[q] : at[q] + 1, :])
            pivots.append(inv)
            scaled = lead[q] * inv
            below = [jnp.where(sub > at[q], cols[q][0], 0.0)] + cols[q][1:]
            for t in range(q + 1, GROUP):
                ratio = wide(cols[t][0][at[q] : at[q] + 1, :]) * inv
                weight = wide(cols[q][0][at[t] : at[t] + 1, :])
                cols[t] = [cols[t][i] - below[i] * ratio for i in range(len(below))]
                lead[t] = lead[t] - weight * scaled
            for i in range(len(below)):
                rows[v0 + i] = rows[v0 + i] - below[i] * scaled
    out = []
    for v in range(nv):
        scale = pivots[8 * v]
        for s in range(1, 8):
            scale = jnp.where(sub == s, pivots[8 * v + s], scale)
        out.append(rows[v] * jnp.sqrt(scale))
    return jnp.concatenate(out, axis=0)


def factor_diag(d_ref, w_ref, base):
    ri = lax.broadcasted_iota(jnp.int32, (NB, NB), 0)
    ci = lax.broadcasted_iota(jnp.int32, (NB, NB), 1)
    w_ref[...] = jnp.where(ri == ci, 1.0, 0.0)
    cb = lax.broadcasted_iota(jnp.int32, (SB, NB), 1)
    rb = lax.broadcasted_iota(jnp.int32, (SB, NB), 0)
    block = pl.ds(base, NB)
    for lo in range(0, NB, SB):
        hi = lo + SB
        here = pl.ds(base + lo, SB)
        strip = d_ref[here, block]
        small = factor_small(strip[:, lo:hi])
        both = mm(small[:, SB:], jnp.concatenate([strip, w_ref[lo:hi, :]], axis=1), 1, 0)
        up = jnp.where(cb >= rb + lo, both[:, :NB], 0.0)
        inv = jnp.where(cb <= rb + lo, both[:, NB:], 0.0)
        d_ref[here, block] = up
        w_ref[lo:hi, :] = inv
        if hi < NB:
            update = mm(up[:, hi:], jnp.concatenate([up, inv], axis=1), 0, 0)
            d_ref[pl.ds(base + hi, NB - hi), block] -= update[:, :NB]
            w_ref[hi:, :] -= update[:, NB:]


def factor_all(n, u_ref, w_ref):
    if n == NB:
        factor_diag(u_ref, w_ref.at[0], 0)
        return

    def step(p, carry):
        factor_diag(u_ref, w_ref.at[p], pl.multiple_of(p * NB, NB))
        for lo in range(0, n - NB, NB):

            @pl.when(p == lo // NB)
            def _():
                hi = lo + NB
                right = mm(w_ref[lo // NB], u_ref[lo:hi, hi:], 1, 0)
                u_ref[lo:hi, hi:] = right
                for q in range(hi, n, NB):
                    own = right[:, q - hi : q - hi + NB]
                    u_ref[q : q + NB, q:] -= mm(own, right[:, q - hi :], 0, 0)

        return carry

    lax.fori_loop(0, n // NB, step, 0)
    for lo in range(NB, n, NB):
        u_ref[lo : lo + NB, :lo] = jnp.zeros((NB, lo), F32)


def chol_kernel(n, a_ref, u_ref, w_ref):
    u_ref[...] = a_ref[...]
    factor_all(n, u_ref, w_ref)


def cholesky_upper(a, name):
    n = a.shape[0]
    return call(
        partial(chol_kernel, n),
        name,
        15,
        out_shape=(
            jax.ShapeDtypeStruct((n, n), F32),
            jax.ShapeDtypeStruct((n // NB, NB, NB), F32),
        ),
    )(a)


def one_hot(pos_row, n):
    ids = lax.broadcasted_iota(jnp.int32, (n, pos_row.shape[1]), 0)
    return jnp.where(ids == pos_row, 1.0, 0.0).astype(BF16)


CORNER = (((0, 0), (0, 1), (1, 1), (2, 0), (3, 0)), ((1, 2), (2, 2), (1, 3), (2, 3), (3, 3)))


def pack_kernel(at_ref, pos_ref, f_ref, o_ref):
    on_top = at_ref[0] == 0
    pivot_cols = at_ref[1] < 2
    inner = jnp.logical_not(jnp.logical_or(on_top, pivot_cols))

    for h in range(2):

        @pl.when(jnp.logical_and(on_top, at_ref[1] == h))
        def _():
            for y in range(4):
                for p in range(KEYS):
                    for t in range(5):
                        at = (p * 5 + t) * 8
                        rb, cb = CORNER[h][at // 128]
                        row = rb * NB + y * 64 + at % 64
                        lane = (cb - 2 * h) * NB + (at % 128) // 64 * 128
                        o_ref[y, 0, p, t * 8 : t * 8 + 8, :] = f_ref[
                            0, row : row + 8, lane : lane + 128
                        ]

    @pl.when(jnp.logical_and(on_top, jnp.logical_not(pivot_cols)))
    def _():
        place = one_hot(pos_ref[0, 2:3, :], BLK)
        out = sum(mm_bf(part, place, 1, 1) for part in split3(f_ref[0]))
        for y in range(4):
            for p in range(KEYS):
                o_ref[y, 0, p] = out[p * 64 : (p + 1) * 64, y * 128 : (y + 1) * 128]

    def store(b, total):
        for y in range(4):
            for p in range(KEYS):
                o_ref[y, 0, p, b * 32 : (b + 1) * 32, :] = total[
                    p * 32 : (p + 1) * 32, y * 128 : (y + 1) * 128
                ]

    def by_row(b):
        place_row = one_hot(pos_ref[0, b : b + 1, :], BLK)
        return [mm_bf(place_row, part, 1, 0) for part in split3(f_ref[0, b * BLK : (b + 1) * BLK, :])]

    @pl.when(jnp.logical_and(jnp.logical_not(on_top), pivot_cols))
    def _():
        for b in range(2):
            store(b, sum(by_row(b)))

    @pl.when(inner)
    def _():
        place_col = one_hot(pos_ref[0, 2:3, :], BLK)
        for b in range(2):
            store(b, sum(mm_bf(place_col, row.astype(BF16), 1, 1) for row in by_row(b)))


def chol_gathered_kernel(at_ref, a_ref, u_ref, w_ref):
    for yy in range(4):
        back = (at_ref[0] - yy) & 3
        for pc in range(KEYS):
            for t in range(5):
                at = (pc * 5 + t) * 8
                blk, q, i = at // 128, (at % 128) // 64, at % 64
                for h in range(2):
                    rb, cb = CORNER[h][blk]
                    row = rb * NB + yy * 64 + i
                    lane = cb * NB + q * 128
                    u_ref[row : row + 8, lane : lane + 128] = a_ref[pc, back, h, t * 8 : t * 8 + 8]
    for cb in (2, 3):
        u_ref[0:NB, cb * NB : (cb + 1) * NB] = u_ref[cb * NB : (cb + 1) * NB, 0:NB].T
    factor_all(u_ref.shape[0], u_ref, w_ref)


def pair(ref, rows, cols):
    return ref[0, rows, cols], ref[1, rows, cols]


def put(ref, rows, cols, value):
    ref[0, rows, cols], ref[1, rows, cols] = split2(value)


def rows_kernel(at_ref, u_ref, w_ref, x_ref, rxs_ref, o_ref, rx_ref, low_ref, inv_ref):
    step = pl.program_id(0)
    panels = u_ref.shape[0] // NB
    every = slice(None)
    strip = pl.ds(pl.multiple_of(at_ref[1] * 64, 64), 64)

    @pl.when(step == 0)
    def _():
        for p in range(panels):
            now, done = slice(p * NB, (p + 1) * NB), slice(0, p * NB)
            put(inv_ref, now, every, w_ref[p])
            if p:
                put(low_ref, now, done, u_ref[done, now].T)
        for yy in range(4):

            @pl.when(at_ref[0] == yy)
            def _():
                o_ref[0] = u_ref[strip, yy * NB : (yy + 1) * NB]

    @pl.when(step > 0)
    def _():
        for p in range(panels):
            now, done = slice(p * NB, (p + 1) * NB), slice(0, p * NB)
            cur = jnp.concatenate(
                [x_ref[4 * p : 4 * p + 4, t].reshape(NB, 128) for t in range(2)], axis=1
            )
            if p:
                cur = cur - mm3(pair(low_ref, now, done), pair(rxs_ref, done, every), 1, 0)
            cur = mm3(pair(inv_ref, now, every), split2(cur), 1, 0)
            rx_ref[now, :] = cur
            put(rxs_ref, now, every, cur)
        o_ref[0] = rx_ref[strip, :]


def schur_kernel(at_ref, u_ref, w_ref, y_ref, rxs_ref, c_ref, s_ref, ry_ref):
    step = pl.program_id(0)
    panels = u_ref.shape[0] // NB
    every = slice(None)

    @pl.when(step == 0)
    def _():
        for p in range(panels):
            now, done = slice(p * NB, (p + 1) * NB), slice(0, p * NB)
            cur = jnp.concatenate(
                [
                    y_ref[(at_ref[0] - (2 * p + t)) & 3, :, (2 * p + t) // 4].reshape(448, 128)
                    for t in range(2)
                ],
                axis=1,
            )
            if p:
                cur = cur - mm3(pair(ry_ref, every, done), split2(u_ref[done, now]), 1, 0)
            put(ry_ref, every, now, mm3(split2(cur), split2(w_ref[p]), 1, 1))

    @pl.when(step > 0)
    def _():
        prod = mm3(pair(ry_ref, every, every), pair(rxs_ref, every, every), 1, 0)
        c0 = c_ref[0, 2:, 0:32, :].reshape(448, 128) - prod[:, :128]
        c1 = c_ref[0, 2:, 32:64, :].reshape(448, 128) - prod[:, 128:]
        lane = lax.broadcasted_iota(jnp.int32, (448, 128), 1)
        s_ref[0] = jnp.where(lane < 64, c0, pltpu.roll(c1, 64, 1))
        s_ref[1] = jnp.where(lane < 64, pltpu.roll(c0, 64, 1), c1)


def unpack_kernel(src_ref, r_ref, o_ref):
    for k in range(2):
        wide = jnp.concatenate([r_ref[2 * yy + k] for yy in range(4)], axis=1)
        place = one_hot_rows(src_ref[k], 1024)
        o_ref[k] = sum(mm_bf(place, part, 1, 1) for part in split3(wide))


def one_hot_rows(src_col, n):
    ids = lax.broadcasted_iota(jnp.int32, (src_col.shape[0], n), 1)
    return jnp.where(ids == src_col, 1.0, 0.0).astype(BF16)


def merge_kernel(core_ref, tx_ref, ty_ref, s_ref, g_ref, p_ref, o_ref, part_ref, ey_ref):
    tile = pl.program_id(0)

    @pl.when(tile == 0)
    def _():
        for k in range(2):
            ey_ref[k] = one_hot(ty_ref[k], 768)
        core = core_ref[0]
        part_ref[core, 0], part_ref[core, 1] = split2(s_ref[0])
        part_ref[1 - core, 0], part_ref[1 - core, 1] = split2(g_ref[...])

    acc = p_ref[...]
    for k in range(2):
        ex = one_hot(tx_ref[k] - tile * NB, NB)
        for i in range(2):
            half = mm_bf(ex, part_ref[k, i], 1, 1)
            acc = acc + mm_bf(half.astype(BF16), ey_ref[k], 1, 1)
    o_ref[...] = acc


def final_kernel(flag_ref, w_ref, m_ref, row_ref, col_ref, o_ref, f_ref, rc_ref):
    tile = pl.program_id(0)
    inv = split2(w_ref[0])

    @pl.when(tile == 0)
    def _():
        rc_ref[0], rc_ref[1] = split2(mm3(inv, split2(col_ref[...]), 1, 0))

    rows = mm3(split2(row_ref[...]), inv, 1, 1)
    f_ref[...] = rows
    out = m_ref[...] - mm3(split2(rows), (rc_ref[0], rc_ref[1]), 1, 0)
    lane = lax.broadcasted_iota(jnp.int32, out.shape, 1)
    keep_row = jnp.logical_or(flag_ref[0] != 0, tile > 0)
    keep = jnp.logical_and(keep_row, jnp.logical_or(flag_ref[1] != 0, lane >= NB))
    o_ref[...] = jnp.where(keep, out, 0.0)


def smem():
    return pl.BlockSpec(memory_space=pltpu.SMEM)


def whole(shape):
    return pl.BlockSpec(shape, lambda *_: (0,) * len(shape))


def local(child_fronts, parent_front, child_map):
    r = lax.axis_index("row")
    c = lax.axis_index("col")
    core = r % 2
    y = r // 2
    nblk = child_map.shape[1] // BLK

    maps = child_map.reshape(2 * nblk, BLK)
    keys = maps // 768
    hot = (keys[:, :, None] == jnp.arange(KEYS, dtype=jnp.int32)).astype(BF16)
    lower = (jnp.arange(BLK)[:, None] >= jnp.arange(BLK)[None, :]).astype(BF16)
    counts = jnp.einsum("ef,bfk->bek", lower, hot, preferred_element_type=F32)
    rank = jnp.sum(counts * hot.astype(F32), axis=2).astype(jnp.int32) - 1
    pos = (keys * 32 + rank).reshape(2, nblk, BLK)
    maps = maps.reshape(2, nblk, BLK)

    pos_c = lax.dynamic_slice_in_dim(pos, jnp.maximum(c - 2, 0), 1, axis=1)
    pos_r = lax.dynamic_slice_in_dim(pos, jnp.maximum(2 * r - 2, 0), 2, axis=1)

    shifts = [[(i, (i + 2 * s) % 8) for i in range(8)] for s in (1, 2, 3)]

    def gather_y(x):
        return jnp.stack([x] + [lax.ppermute(x, "row", pairs) for pairs in shifts])

    def swap(x, axes):
        return lax.all_to_all(x, axes, split_axis=0, concat_axis=0, tiled=True)

    def repeat(x, axes, parts):
        x = lax.optimization_barrier(x)
        return swap(jnp.broadcast_to(x[None], (parts, *x.shape)), axes)

    at = jnp.stack([y, c])
    packed = call(
        pack_kernel,
        "pack",
        8,
        grid=(2,),
        in_specs=[
            smem(),
            pl.BlockSpec((1, 3, BLK), lambda k: (k, 0, 0)),
            pl.BlockSpec((1, 1024, BLK), lambda k: (k, 0, 0)),
        ],
        out_specs=pl.BlockSpec((4, 1, KEYS, 64, 128), lambda k: (0, k, 0, 0, 0)),
        out_shape=jax.ShapeDtypeStruct((4, 2, KEYS, 64, 128), F32),
    )(jnp.stack([r, c]), jnp.concatenate([pos_r, pos_c], axis=1), child_fronts)
    arrived = swap(packed.reshape(8 * KEYS, 64, 128), ("row", "col")).reshape(8, KEYS, 64, 128)
    spread = gather_y(arrived[0, :2, :40])
    pieces = lax.all_gather(spread, "col")
    own_x, _ = lax.optimization_barrier((arrived[0, 2:], spread))
    panel_x = lax.all_gather(own_x, "col")
    upper, inverses = call(
        chol_gathered_kernel,
        "child_factor",
        64,
        in_specs=[smem(), whole((KEYS, 4, 2, 40, 128))],
        out_shape=(
            jax.ShapeDtypeStruct((1024, 1024), F32),
            jax.ShapeDtypeStruct((4, NB, NB), F32),
        ),
    )(at, pieces)
    mine_y = arrived[1:, :2]
    shifted_y = [lax.ppermute(mine_y, "row", pairs) for pairs in shifts]

    factor_x, outgoing = call(
        rows_kernel,
        "rows",
        20,
        grid=(8,),
        in_specs=[
            smem(),
            whole((1024, 1024)),
            whole((4, NB, NB)),
            pl.BlockSpec((KEYS, 2, 64, 128), lambda g: (0, jnp.maximum(g, 1) - 1, 0, 0)),
        ],
        out_specs=(
            pl.BlockSpec((2, 1024, NB), lambda g: (0, 0, jnp.maximum(g, 1) - 1)),
            pl.BlockSpec((1, 64, NB), lambda g: (g, 0, 0)),
        ),
        out_shape=(
            jax.ShapeDtypeStruct((2, 1024, 1792), BF16),
            jax.ShapeDtypeStruct((8, 64, NB), F32),
        ),
        scratch_shapes=[
            pltpu.VMEM((1024, NB), F32),
            pltpu.VMEM((2, 1024, 1024), BF16),
            pltpu.VMEM((2, 1024, NB), BF16),
        ],
    )(at, upper, inverses, panel_x)
    factor_x, *shifted_y = lax.optimization_barrier((factor_x, *shifted_y))
    panel_y = jnp.stack([mine_y, *shifted_y])
    landed = swap(outgoing, "row")
    schur = call(
        schur_kernel,
        "schur",
        18,
        grid=(8,),
        in_specs=[
            smem(),
            whole((1024, 1024)),
            whole((4, NB, NB)),
            whole((4, 7, 2, 64, 128)),
            pl.BlockSpec((2, 1024, NB), lambda g: (0, 0, jnp.maximum(g, 1) - 1)),
            pl.BlockSpec((1, KEYS, 64, 128), lambda g: (jnp.maximum(g, 1), 0, 0, 0)),
        ],
        out_specs=pl.BlockSpec((2, 448, 128), lambda g: (0, 0, jnp.maximum(g, 1) - 1)),
        out_shape=jax.ShapeDtypeStruct((2, 448, 896), F32),
        scratch_shapes=[pltpu.VMEM((2, 448, 1024), BF16)],
    )(at, upper, inverses, panel_y, factor_x, arrived)

    got = lax.ppermute(
        lax.dynamic_index_in_dim(schur, 1 - core, 0, keepdims=False),
        "row",
        [(i, i ^ 1) for i in range(8)],
    )

    spot = (pos_r // 128) * NB + jnp.arange(2, dtype=jnp.int32)[None, :, None] * 128 + pos_r % 128
    natural = jnp.broadcast_to(jnp.arange(1024, dtype=jnp.int32), (2, 1024))
    spot = jnp.where(r == 0, natural, spot.reshape(2, 1024))
    def sorted_maps(start, count):
        ids = start + jnp.arange(count, dtype=jnp.int32)
        return jnp.sum(
            jnp.where(pos[:, :, :, None] == ids, maps[:, :, :, None], 0), axis=2, dtype=jnp.int32
        )

    to_rows = sorted_maps(r * 64, 64).reshape(2, 1, 896) - r * 1536
    to_cols = sorted_maps(c * 32, 32).reshape(2, 1, 448) - c * 768
    merged = pl.pallas_call(
        merge_kernel,
        name="merge",
        cost_estimate=pl.CostEstimate(flops=19 * 10**9, transcendentals=0, bytes_accessed=1 << 20),
        compiler_params=pltpu.CompilerParams(vmem_limit_bytes=VMEM_LIMIT),
        grid_spec=pltpu.PrefetchScalarGridSpec(
            num_scalar_prefetch=1,
            grid=(6,),
            in_specs=[
                whole((2, 1, 896)),
                whole((2, 1, 448)),
                pl.BlockSpec((1, 448, 896), lambda t, which: (which[0], 0, 0)),
                whole((448, 896)),
                pl.BlockSpec((NB, 768), lambda t, which: (t, 0)),
            ],
            out_specs=pl.BlockSpec((NB, 768), lambda t, which: (t, 0)),
            scratch_shapes=[pltpu.VMEM((2, 2, 448, 896), BF16), pltpu.VMEM((2, 768, 448), BF16)],
        ),
        out_shape=jax.ShapeDtypeStruct((1536, 768), F32),
    )(core[None], to_rows, to_cols, schur, got, parent_front)
    merged, landed = lax.optimization_barrier((merged, landed))
    child_factor = call(
        unpack_kernel, "unpack", 6, out_shape=jax.ShapeDtypeStruct((2, 1024, 64), F32)
    )(spot[:, :, None], landed)

    top = repeat(swap(merged[:NB].reshape(8, 32, 768), "row")[0], "row", 8).reshape(NB, 768)
    side = jnp.concatenate([merged[:, :NB], top[:, :NB]]).reshape(KEYS, 112, NB)
    side, child_factor = lax.optimization_barrier((swap(side, "col")[0], child_factor))
    left = repeat(side, "col", KEYS).reshape(1792, NB)
    _, parent_inverse = cholesky_upper(left[1536:], "parent_factor")
    schur_out, rows_out = call(
        final_kernel,
        "final",
        10,
        grid=(6,),
        in_specs=[
            smem(),
            whole((1, NB, NB)),
            pl.BlockSpec((NB, 768), lambda t: (t, 0)),
            pl.BlockSpec((NB, NB), lambda t: (t, 0)),
            whole((NB, 768)),
        ],
        out_specs=(
            pl.BlockSpec((NB, 768), lambda t: (t, 0)),
            pl.BlockSpec((NB, NB), lambda t: (t, 0)),
        ),
        out_shape=(
            jax.ShapeDtypeStruct((1536, 768), F32),
            jax.ShapeDtypeStruct((1536, NB), F32),
        ),
        scratch_shapes=[pltpu.VMEM((2, NB, 768), BF16)],
    )(jnp.stack([r, c]), parent_inverse, merged, left, top)
    parent_factor = lax.dynamic_slice_in_dim(rows_out, c * 16, 16, axis=1)
    return child_factor, parent_factor, schur_out


def solution(mesh):
    return jax.shard_map(
        local,
        mesh=mesh,
        in_specs=(P(None, "row", "col"), P("row", "col"), P()),
        out_specs=(P(None, "row", "col"), P("row", "col"), P("row", "col")),
        check_vma=False,
    )
```

```python
from functools import partial

import jax
import jax.numpy as jnp
from jax import lax
from jax.experimental import pallas as pl
from jax.experimental.pallas import tpu as pltpu
from jax.sharding import PartitionSpec as P

F32 = jnp.float32
BF16 = jnp.bfloat16
NB = 256
SB = 64
GROUP = 4
BLK = 512
KEYS = 16
HIGHEST = lax.Precision.HIGHEST
VMEM_LIMIT = 56 << 20


def mm(a, b, ca, cb):
    return lax.dot_general(
        a, b, (((ca,), (cb,)), ((), ())), precision=HIGHEST, preferred_element_type=F32
    )


def mm_bf(a, b, ca, cb):
    return lax.dot_general(a, b, (((ca,), (cb,)), ((), ())), preferred_element_type=F32)


def split2(x):
    hi = x.astype(BF16)
    return hi, (x - hi.astype(F32)).astype(BF16)


def mm3(a, b, ca, cb):
    return mm_bf(a[0], b[0], ca, cb) + (mm_bf(a[0], b[1], ca, cb) + mm_bf(a[1], b[0], ca, cb))


def split3(x):
    hi = x.astype(BF16)
    rest = x - hi.astype(F32)
    mid = rest.astype(BF16)
    low = (rest - mid.astype(F32)).astype(BF16)
    return hi, mid, low


def call(kernel, name, us, **kw):
    return pl.pallas_call(
        kernel,
        name=name,
        cost_estimate=pl.CostEstimate(flops=us * 10**9, transcendentals=0, bytes_accessed=1 << 20),
        compiler_params=pltpu.CompilerParams(vmem_limit_bytes=VMEM_LIMIT),
        **kw,
    )


def factor_small(diag):
    n = SB
    ri = lax.broadcasted_iota(jnp.int32, (n, n), 0)
    ci = lax.broadcasted_iota(jnp.int32, (n, n), 1)
    full = jnp.concatenate([diag, jnp.where(ri == ci, 1.0, 0.0)], axis=1)
    nv = n // 8
    rows = [full[8 * v : 8 * v + 8, :] for v in range(nv)]
    sub = lax.broadcasted_iota(jnp.int32, (8, 2 * n), 0)
    wide = lambda x: jnp.broadcast_to(x, (8, 2 * n))
    pivots = []
    for j0 in range(0, n, GROUP):
        v0 = j0 // 8
        cols = [[wide(rows[v][:, j0 + q : j0 + q + 1]) for v in range(v0, nv)] for q in range(GROUP)]
        at = [(j0 + q) % 8 for q in range(GROUP)]
        lead = [wide(rows[v0][at[q] : at[q] + 1, :]) for q in range(GROUP)]
        for q in range(GROUP):
            inv = 1.0 / wide(cols[q][0][at[q] : at[q] + 1, :])
            pivots.append(inv)
            scaled = lead[q] * inv
            below = [jnp.where(sub > at[q], cols[q][0], 0.0)] + cols[q][1:]
            for t in range(q + 1, GROUP):
                ratio = wide(cols[t][0][at[q] : at[q] + 1, :]) * inv
                weight = wide(cols[q][0][at[t] : at[t] + 1, :])
                cols[t] = [cols[t][i] - below[i] * ratio for i in range(len(below))]
                lead[t] = lead[t] - weight * scaled
            for i in range(len(below)):
                rows[v0 + i] = rows[v0 + i] - below[i] * scaled
    out = []
    for v in range(nv):
        scale = pivots[8 * v]
        for s in range(1, 8):
            scale = jnp.where(sub == s, pivots[8 * v + s], scale)
        out.append(rows[v] * jnp.sqrt(scale))
    return jnp.concatenate(out, axis=0)


def factor_diag(d_ref, w_ref, base):
    ri = lax.broadcasted_iota(jnp.int32, (NB, NB), 0)
    ci = lax.broadcasted_iota(jnp.int32, (NB, NB), 1)
    w_ref[...] = jnp.where(ri == ci, 1.0, 0.0)
    cb = lax.broadcasted_iota(jnp.int32, (SB, NB), 1)
    rb = lax.broadcasted_iota(jnp.int32, (SB, NB), 0)
    block = pl.ds(base, NB)
    for lo in range(0, NB, SB):
        hi = lo + SB
        here = pl.ds(base + lo, SB)
        strip = d_ref[here, block]
        small = factor_small(strip[:, lo:hi])
        both = mm(small[:, SB:], jnp.concatenate([strip, w_ref[lo:hi, :]], axis=1), 1, 0)
        up = jnp.where(cb >= rb + lo, both[:, :NB], 0.0)
        inv = jnp.where(cb <= rb + lo, both[:, NB:], 0.0)
        d_ref[here, block] = up
        w_ref[lo:hi, :] = inv
        if hi < NB:
            update = mm(up[:, hi:], jnp.concatenate([up, inv], axis=1), 0, 0)
            d_ref[pl.ds(base + hi, NB - hi), block] -= update[:, :NB]
            w_ref[hi:, :] -= update[:, NB:]


def factor_all(n, u_ref, w_ref):
    if n == NB:
        factor_diag(u_ref, w_ref.at[0], 0)
        return

    def step(p, carry):
        factor_diag(u_ref, w_ref.at[p], pl.multiple_of(p * NB, NB))
        for lo in range(0, n - NB, NB):

            @pl.when(p == lo // NB)
            def _():
                hi = lo + NB
                right = mm(w_ref[lo // NB], u_ref[lo:hi, hi:], 1, 0)
                u_ref[lo:hi, hi:] = right
                for q in range(hi, n, NB):
                    own = right[:, q - hi : q - hi + NB]
                    u_ref[q : q + NB, q:] -= mm(own, right[:, q - hi :], 0, 0)

        return carry

    lax.fori_loop(0, n // NB, step, 0)
    for lo in range(NB, n, NB):
        u_ref[lo : lo + NB, :lo] = jnp.zeros((NB, lo), F32)


def chol_kernel(n, a_ref, u_ref, w_ref):
    u_ref[...] = a_ref[...]
    factor_all(n, u_ref, w_ref)


def cholesky_upper(a, name):
    n = a.shape[0]
    return call(
        partial(chol_kernel, n),
        name,
        15,
        out_shape=(
            jax.ShapeDtypeStruct((n, n), F32),
            jax.ShapeDtypeStruct((n // NB, NB, NB), F32),
        ),
    )(a)


def one_hot(pos_row, n):
    ids = lax.broadcasted_iota(jnp.int32, (n, pos_row.shape[1]), 0)
    return jnp.where(ids == pos_row, 1.0, 0.0).astype(BF16)


CORNER = (((0, 0), (0, 1), (1, 1), (2, 0), (3, 0)), ((1, 2), (2, 2), (1, 3), (2, 3), (3, 3)))


def pack_kernel(at_ref, pos_ref, f_ref, o_ref):
    on_top = at_ref[0] == 0
    pivot_cols = at_ref[1] < 2
    inner = jnp.logical_not(jnp.logical_or(on_top, pivot_cols))

    for h in range(2):

        @pl.when(jnp.logical_and(on_top, at_ref[1] == h))
        def _():
            for y in range(4):
                for p in range(KEYS):
                    for t in range(5):
                        at = (p * 5 + t) * 8
                        rb, cb = CORNER[h][at // 128]
                        row = rb * NB + y * 64 + at % 64
                        lane = (cb - 2 * h) * NB + (at % 128) // 64 * 128
                        o_ref[y, 0, p, t * 8 : t * 8 + 8, :] = f_ref[
                            0, row : row + 8, lane : lane + 128
                        ]

    @pl.when(jnp.logical_and(on_top, jnp.logical_not(pivot_cols)))
    def _():
        place = one_hot(pos_ref[0, 2:3, :], BLK)
        out = sum(mm_bf(part, place, 1, 1) for part in split3(f_ref[0]))
        for y in range(4):
            for p in range(KEYS):
                o_ref[y, 0, p] = out[p * 64 : (p + 1) * 64, y * 128 : (y + 1) * 128]

    def store(b, total):
        for y in range(4):
            for p in range(KEYS):
                o_ref[y, 0, p, b * 32 : (b + 1) * 32, :] = total[
                    p * 32 : (p + 1) * 32, y * 128 : (y + 1) * 128
                ]

    def by_row(b):
        place_row = one_hot(pos_ref[0, b : b + 1, :], BLK)
        return [mm_bf(place_row, part, 1, 0) for part in split3(f_ref[0, b * BLK : (b + 1) * BLK, :])]

    @pl.when(jnp.logical_and(jnp.logical_not(on_top), pivot_cols))
    def _():
        for b in range(2):
            store(b, sum(by_row(b)))

    @pl.when(inner)
    def _():
        place_col = one_hot(pos_ref[0, 2:3, :], BLK)
        for b in range(2):
            store(b, sum(mm_bf(place_col, row.astype(BF16), 1, 1) for row in by_row(b)))


def chol_gathered_kernel(at_ref, a_ref, u_ref, w_ref):
    for yy in range(4):
        back = (at_ref[0] - yy) & 3
        for pc in range(KEYS):
            for t in range(5):
                at = (pc * 5 + t) * 8
                blk, q, i = at // 128, (at % 128) // 64, at % 64
                for h in range(2):
                    rb, cb = CORNER[h][blk]
                    row = rb * NB + yy * 64 + i
                    lane = cb * NB + q * 128
                    u_ref[row : row + 8, lane : lane + 128] = a_ref[pc, back, h, t * 8 : t * 8 + 8]
    for cb in (2, 3):
        u_ref[0:NB, cb * NB : (cb + 1) * NB] = u_ref[cb * NB : (cb + 1) * NB, 0:NB].T
    factor_all(u_ref.shape[0], u_ref, w_ref)


def pair(ref, rows, cols):
    return ref[0, rows, cols], ref[1, rows, cols]


def put(ref, rows, cols, value):
    ref[0, rows, cols], ref[1, rows, cols] = split2(value)


def rows_kernel(at_ref, u_ref, w_ref, x_ref, rxs_ref, o_ref, rx_ref, low_ref, inv_ref):
    step = pl.program_id(0)
    panels = u_ref.shape[0] // NB
    every = slice(None)
    strip = pl.ds(pl.multiple_of(at_ref[1] * 64, 64), 64)

    @pl.when(step == 0)
    def _():
        for p in range(panels):
            now, done = slice(p * NB, (p + 1) * NB), slice(0, p * NB)
            put(inv_ref, now, every, w_ref[p])
            if p:
                put(low_ref, now, done, u_ref[done, now].T)

    for p in range(panels):
        now, done = slice(p * NB, (p + 1) * NB), slice(0, p * NB)
        cur = jnp.concatenate([x_ref[4 * p : 4 * p + 4, t].reshape(NB, 128) for t in range(4)], axis=1)
        if p:
            cur = cur - mm3(pair(low_ref, now, done), pair(rxs_ref, done, every), 1, 0)
        cur = mm3(pair(inv_ref, now, every), split2(cur), 1, 0)
        rx_ref[now, :] = cur
        put(rxs_ref, now, every, cur)
    o_ref[1] = rx_ref[strip, NB:]

    @pl.when(step > 0)
    def _():
        o_ref[0] = rx_ref[strip, :NB]

    @pl.when(step == 0)
    def _():
        for yy in range(4):

            @pl.when(at_ref[0] == yy)
            def _():
                o_ref[0] = u_ref[strip, yy * NB : (yy + 1) * NB]


def halves(c0, c1):
    lane = lax.broadcasted_iota(jnp.int32, c0.shape, 1)
    first = jnp.where(lane < 64, c0, pltpu.roll(c1, 64, 1))
    return first, jnp.where(lane < 64, pltpu.roll(c0, 64, 1), c1)


def store_halves(core, mine_ref, other_ref, rows, c0, c1):
    first, second = halves(c0, c1)

    @pl.when(core == 0)
    def _():
        mine_ref[rows, :], other_ref[rows, :] = first, second

    @pl.when(core != 0)
    def _():
        mine_ref[rows, :], other_ref[rows, :] = second, first


def split_kernel(at_ref, c_ref, mine_ref, other_ref):
    c0 = c_ref[0, 2:, 0:32, :].reshape(448, 128)
    c1 = c_ref[0, 2:, 32:64, :].reshape(448, 128)
    store_halves(at_ref[2], mine_ref, other_ref, slice(None), c0, c1)


def schur_kernel(
    at_ref, u_ref, w_ref, y_ref, rp_ref, rxs_ref, c_ref, mine_ref, other_ref, t_ref, ry_ref
):
    step = pl.program_id(0)
    panels = u_ref.shape[0] // NB
    every, cols = slice(None), slice(NB, NB + 448)

    @pl.when(step == 0)
    def _():
        for h in range(2):
            ry_ref[h, :NB, :] = rp_ref[h].astype(F32).T.astype(BF16)
        for p in range(panels):
            now, done = slice(p * NB, (p + 1) * NB), slice(0, p * NB)
            cur = jnp.concatenate(
                [
                    y_ref[(at_ref[0] - (2 * p + t)) & 3, :, (2 * p + t) // 4].reshape(448, 128)
                    for t in range(2)
                ],
                axis=1,
            )
            if p:
                cur = cur - mm3(pair(ry_ref, cols, done), split2(u_ref[done, now]), 1, 0)
            put(ry_ref, cols, now, mm3(split2(cur), split2(w_ref[p]), 1, 1))
        t_ref[:, NB + 448 :] = jnp.zeros((NB, 64), F32)
        t_ref[:, : NB + 448] = -mm3(pair(ry_ref, slice(0, NB), every), pair(ry_ref, every, every), 1, 1)

    @pl.when(step > 0)
    def _():
        prod = -mm3(pair(ry_ref, every, every), pair(rxs_ref, every, every), 1, 0)
        store_halves(
            at_ref[2], mine_ref, other_ref, slice(0, NB), prod[:NB, :128], prod[:NB, 128:]
        )
        c0 = c_ref[0, 2:, 0:32, :].reshape(448, 128) + prod[cols, :128]
        c1 = c_ref[0, 2:, 32:64, :].reshape(448, 128) + prod[cols, 128:]
        store_halves(at_ref[2], mine_ref, other_ref, cols, c0, c1)


def unpack_kernel(row_ref, pos_ref, r_ref, o_ref):
    for k in range(2):

        @pl.when(row_ref[0] == 0)
        def _():
            for yy in range(4):
                o_ref[k, :, yy * NB : (yy + 1) * NB] = r_ref[2 * yy + k]

        @pl.when(row_ref[0] != 0)
        def _():
            for b in range(2):
                here = slice(b * 128, (b + 1) * 128)
                wide = jnp.concatenate([r_ref[2 * yy + k, :, here] for yy in range(4)], axis=1)
                place = one_hot(pos_ref[k, b : b + 1, :], BLK)
                o_ref[k, :, b * BLK : (b + 1) * BLK] = sum(
                    mm_bf(part, place, 1, 0) for part in split3(wide)
                )


def load_parts(core_ref, s_ref, g_ref, part_ref):
    core = core_ref[0]
    part_ref[core, 0], part_ref[core, 1] = split2(s_ref[...])
    part_ref[1 - core, 0], part_ref[1 - core, 1] = split2(g_ref[...])


def merge_kernel(core_ref, tx_ref, ty_ref, s_ref, g_ref, p_ref, o_ref, part_ref, ey_ref):
    tile = pl.program_id(0)

    @pl.when(tile == 0)
    def _():
        for k in range(2):
            ey_ref[k] = one_hot(ty_ref[k], ey_ref.shape[1])
        load_parts(core_ref, s_ref, g_ref, part_ref)

    acc = p_ref[...]
    for k in range(2):
        ex = one_hot(tx_ref[k] - tile * NB, NB)
        for i in range(2):
            half = mm_bf(ex, part_ref[k, i], 1, 1)
            acc = acc + mm_bf(half.astype(BF16), ey_ref[k], 1, 1)
    o_ref[...] = acc


def final_kernel(
    core_ref, tx_ref, ty_ref, s_ref, g_ref, t_ref, tg_ref, w_ref, p_ref, row_ref, col_ref,
    o_ref, f_ref, part_ref, ey_ref, rc_ref, rt_ref,
):
    tile = pl.program_id(0)
    inv = split2(w_ref[0])

    @pl.when(tile == 0)
    def _():
        for k in range(2):
            ey_ref[k] = one_hot(ty_ref[k], 768)
        load_parts(core_ref, s_ref, g_ref, part_ref)
        top = col_ref[...]
        core = core_ref[0]
        for ref, k in ((t_ref, core), (tg_ref, 1 - core)):
            for part in split2(ref[:, NB : NB + 448]):
                top = top + mm_bf(part, ey_ref[k], 1, 1)
        rc_ref[0], rc_ref[1] = split2(mm3(inv, split2(top), 1, 0))

    acc = p_ref[...]
    left = row_ref[...]
    for k in range(2):
        ex = one_hot(tx_ref[k] - tile * NB, NB)
        for i in range(2):
            half = mm_bf(ex, part_ref[k, i], 1, 1)
            left = left + half[:, :NB]
            acc = acc + mm_bf(half[:, NB:].astype(BF16), ey_ref[k], 1, 1)
    rows = mm3(split2(left), inv, 1, 1)
    rt_ref[...] = rows.T
    f_ref[...] = rt_ref[pl.ds(pl.multiple_of(core_ref[2] * 16, 16), 16), :]
    out = acc - mm3(split2(rows), (rc_ref[0], rc_ref[1]), 1, 0)
    lane = lax.broadcasted_iota(jnp.int32, out.shape, 1)
    keep_row = jnp.logical_or(core_ref[1] != 0, tile > 0)
    keep = jnp.logical_and(keep_row, jnp.logical_or(core_ref[2] != 0, lane >= NB))
    o_ref[...] = jnp.where(keep, out, 0.0)


def call_core(kernel, name, us, grid, in_specs, out_specs, scratch_shapes, out_shape):
    return pl.pallas_call(
        kernel,
        name=name,
        cost_estimate=pl.CostEstimate(flops=us * 10**9, transcendentals=0, bytes_accessed=1 << 20),
        compiler_params=pltpu.CompilerParams(vmem_limit_bytes=VMEM_LIMIT),
        grid_spec=pltpu.PrefetchScalarGridSpec(
            num_scalar_prefetch=1,
            grid=grid,
            in_specs=in_specs,
            out_specs=out_specs,
            scratch_shapes=scratch_shapes,
        ),
        out_shape=out_shape,
    )


def smem():
    return pl.BlockSpec(memory_space=pltpu.SMEM)


def whole(shape):
    return pl.BlockSpec(shape, lambda *_: (0,) * len(shape))


def local(child_fronts, parent_front, child_map):
    r = lax.axis_index("row")
    c = lax.axis_index("col")
    core = r % 2
    y = r // 2
    nblk = child_map.shape[1] // BLK

    maps = child_map.reshape(2 * nblk, BLK)
    keys = maps // 768
    hot = (keys[:, :, None] == jnp.arange(KEYS, dtype=jnp.int32)).astype(BF16)
    lower = (jnp.arange(BLK)[:, None] >= jnp.arange(BLK)[None, :]).astype(BF16)
    counts = jnp.einsum("ef,bfk->bek", lower, hot, preferred_element_type=F32)
    rank = jnp.sum(counts * hot.astype(F32), axis=2).astype(jnp.int32) - 1
    pos = (keys * 32 + rank).reshape(2, nblk, BLK)
    maps = maps.reshape(2, nblk, BLK)

    pos_own = lax.dynamic_index_in_dim(pos, core, 0, keepdims=False)
    maps_own = lax.dynamic_index_in_dim(maps, core, 0, keepdims=False)
    pos_c = lax.dynamic_slice_in_dim(pos, jnp.maximum(c - 2, 0), 1, axis=1)
    pos_r = lax.dynamic_slice_in_dim(pos, jnp.maximum(2 * r - 2, 0), 2, axis=1)

    def sorted_maps(start, count):
        ids = start + jnp.arange(count, dtype=jnp.int32)
        return jnp.sum(
            jnp.where(pos[:, :, :, None] == ids, maps[:, :, :, None], 0), axis=2, dtype=jnp.int32
        )

    to_rows = sorted_maps(r * 64, 64).reshape(2, 1, 896) - r * 1536
    to_cols = sorted_maps(c * 32, 32).reshape(2, 1, 448) - c * 768
    shifts = [[(i, (i + 2 * s) % 8) for i in range(8)] for s in (1, 2, 3)]

    def gather_y(x):
        return jnp.stack([x] + [lax.ppermute(x, "row", pairs) for pairs in shifts])

    def swap(x, axes):
        return lax.all_to_all(x, axes, split_axis=0, concat_axis=0, tiled=True)

    def repeat(x, axes, parts):
        x = lax.optimization_barrier(x)
        return swap(jnp.broadcast_to(x[None], (parts, *x.shape)), axes)

    at = jnp.stack([y, c, core])
    packed = call(
        pack_kernel,
        "pack",
        8,
        grid=(2,),
        in_specs=[
            smem(),
            pl.BlockSpec((1, 3, BLK), lambda k: (k, 0, 0)),
            pl.BlockSpec((1, 1024, BLK), lambda k: (k, 0, 0)),
        ],
        out_specs=pl.BlockSpec((4, 1, KEYS, 64, 128), lambda k: (0, k, 0, 0, 0)),
        out_shape=jax.ShapeDtypeStruct((4, 2, KEYS, 64, 128), F32),
    )(jnp.stack([r, c]), jnp.concatenate([pos_r, pos_c], axis=1), child_fronts)
    arrived = swap(packed.reshape(8 * KEYS, 64, 128), ("row", "col")).reshape(8, KEYS, 64, 128)
    spread = gather_y(arrived[0, :2, :40])
    pieces = lax.all_gather(spread, "col")

    pivot_ids = jnp.sum(
        jnp.where(
            pos_own[:, :, None] == jnp.arange(32, dtype=jnp.int32), maps_own[:, :, None], 0
        ),
        axis=1,
        dtype=jnp.int32,
    )
    pick = (pivot_ids[:, :, None] == jnp.arange(NB, dtype=jnp.int32)).astype(F32)
    pivot_x = jnp.einsum("bis,bsp->ip", arrived[0, 2:, :, :32], pick, precision=HIGHEST)
    moved = pivot_x
    for s, pairs in enumerate(shifts):
        got = lax.ppermute(pivot_x, "row", pairs)
        moved = jnp.where(y == s + 1, got, moved)
    moved = jnp.stack([moved[:, :128], moved[:, 128:]])
    own_x, _ = lax.optimization_barrier((jnp.concatenate([moved, arrived[0, 2:]]), spread))
    panel_x = lax.all_gather(own_x, "col")

    raw, raw_other = call(
        split_kernel,
        "split",
        4,
        grid=(7,),
        in_specs=[smem(), pl.BlockSpec((1, KEYS, 64, 128), lambda g: (g + 1, 0, 0, 0))],
        out_specs=[pl.BlockSpec((448, 128), lambda g: (0, g))] * 2,
        out_shape=[jax.ShapeDtypeStruct((448, 896), F32)] * 2,
    )(at, arrived)
    sibling = [(i, i ^ 1) for i in range(8)]
    flags = jnp.stack([core, r, c])
    raw_got = lax.ppermute(raw_other, "row", sibling)

    def merge(tiles, cols, us):
        return call_core(
            merge_kernel,
            "merge",
            us,
            (tiles,),
            [
                whole((2, 1, 896)),
                whole((2, 1, 448)),
                whole((448, 896)),
                whole((448, 896)),
                pl.BlockSpec((NB, cols), lambda t, which: (t, 0)),
            ],
            pl.BlockSpec((NB, cols), lambda t, which: (t, 0)),
            [pltpu.VMEM((2, 2, 448, 896), BF16), pltpu.VMEM((2, cols, 448), BF16)],
            jax.ShapeDtypeStruct((tiles * NB, cols), F32),
        )(flags, to_rows, to_cols, raw, raw_got, parent_front)

    top = swap(merge(1, 768, 6).reshape(8, 32, 768), "row")[0]
    pieces, top, side = lax.optimization_barrier((pieces, top, merge(6, NB, 14)))
    top = repeat(top, "row", 8).reshape(NB, 768)
    upper, inverses = call(
        chol_gathered_kernel,
        "child_factor",
        64,
        in_specs=[smem(), whole((KEYS, 4, 2, 40, 128))],
        out_shape=(
            jax.ShapeDtypeStruct((1024, 1024), F32),
            jax.ShapeDtypeStruct((4, NB, NB), F32),
        ),
    )(at, pieces)
    panel_x, upper, top = lax.optimization_barrier((panel_x, upper, top))
    side = swap(jnp.concatenate([side, top[:, :NB]]).reshape(KEYS, 112, NB), "col")[0]
    mine_y = arrived[1:, :2]
    shifted_y = [lax.ppermute(mine_y, "row", pairs) for pairs in shifts]

    factor_x, outgoing = call(
        rows_kernel,
        "rows",
        24,
        grid=(4,),
        in_specs=[
            smem(),
            whole((1024, 1024)),
            whole((4, NB, NB)),
            pl.BlockSpec((KEYS, 4, 64, 128), lambda g: (0, g, 0, 0)),
        ],
        out_specs=(
            pl.BlockSpec((2, 1024, BLK), lambda g: (0, 0, g)),
            pl.BlockSpec((2, 64, NB), lambda g: (g, 0, 0)),
        ),
        out_shape=(
            jax.ShapeDtypeStruct((2, 1024, 2048), BF16),
            jax.ShapeDtypeStruct((8, 64, NB), F32),
        ),
        scratch_shapes=[
            pltpu.VMEM((1024, BLK), F32),
            pltpu.VMEM((2, 1024, 1024), BF16),
            pltpu.VMEM((2, 1024, NB), BF16),
        ],
    )(at, upper, inverses, panel_x)
    factor_x, side, *shifted_y = lax.optimization_barrier((factor_x, side, *shifted_y))
    left = repeat(side, "col", KEYS).reshape(1792, NB)
    panel_y = jnp.stack([mine_y, *shifted_y])
    schur, other, cross = call(
        schur_kernel,
        "schur",
        25,
        grid=(8,),
        in_specs=[
            smem(),
            whole((1024, 1024)),
            whole((4, NB, NB)),
            whole((4, 7, 2, 64, 128)),
            pl.BlockSpec((2, 1024, NB), lambda g: (0, 0, 0)),
            pl.BlockSpec((2, 1024, NB), lambda g: (0, 0, jnp.maximum(g, 1))),
            pl.BlockSpec((1, KEYS, 64, 128), lambda g: (jnp.maximum(g, 1), 0, 0, 0)),
        ],
        out_specs=(
            pl.BlockSpec((NB + 448, 128), lambda g: (0, jnp.maximum(g, 1) - 1)),
            pl.BlockSpec((NB + 448, 128), lambda g: (0, jnp.maximum(g, 1) - 1)),
            whole((NB, 768)),
        ),
        out_shape=(
            jax.ShapeDtypeStruct((NB + 448, 896), F32),
            jax.ShapeDtypeStruct((NB + 448, 896), F32),
            jax.ShapeDtypeStruct((NB, 768), F32),
        ),
        scratch_shapes=[pltpu.VMEM((2, NB + 448, 1024), BF16)],
    )(at, upper, inverses, panel_y, factor_x, factor_x, arrived)

    cross_got = lax.ppermute(cross, "row", sibling)
    got = lax.ppermute(other, "row", sibling)
    left, outgoing = lax.optimization_barrier((left, outgoing))
    landed = swap(outgoing, "row")

    child_factor = call(
        unpack_kernel,
        "unpack",
        4,
        in_specs=[smem(), whole((2, 2, BLK)), whole((8, 64, NB))],
        out_shape=jax.ShapeDtypeStruct((2, 64, 1024), F32),
    )(r[None], pos_r, landed).swapaxes(1, 2)

    corner = left[1536:] + cross[:, :NB] + cross_got[:, :NB]
    _, parent_inverse = cholesky_upper(corner, "parent_factor")
    schur_out, rows_out = call_core(
        final_kernel,
        "final",
        32,
        (6,),
        [
            whole((2, 1, 896)),
            whole((2, 1, 448)),
            whole((NB + 448, 896)),
            whole((NB + 448, 896)),
            whole((NB, 768)),
            whole((NB, 768)),
            whole((1, NB, NB)),
            pl.BlockSpec((NB, 768), lambda t, which: (t, 0)),
            pl.BlockSpec((NB, NB), lambda t, which: (t, 0)),
            whole((NB, 768)),
        ],
        (
            pl.BlockSpec((NB, 768), lambda t, which: (t, 0)),
            pl.BlockSpec((16, NB), lambda t, which: (0, t)),
        ),
        [
            pltpu.VMEM((2, 2, NB + 448, 896), BF16),
            pltpu.VMEM((2, 768, 448), BF16),
            pltpu.VMEM((2, NB, 768), BF16),
            pltpu.VMEM((NB, NB), F32),
        ],
        (
            jax.ShapeDtypeStruct((1536, 768), F32),
            jax.ShapeDtypeStruct((16, 1536), F32),
        ),
    )(flags, to_rows, to_cols, schur, got, cross, cross_got, parent_inverse, parent_front, left, top)
    return child_factor, rows_out.T, schur_out


def solution(mesh):
    return jax.shard_map(
        local,
        mesh=mesh,
        in_specs=(P(None, "row", "col"), P("row", "col"), P()),
        out_specs=(P(None, "row", "col"), P("row", "col"), P("row", "col")),
        check_vma=False,
    )
```

```python
from functools import partial

import jax
import jax.numpy as jnp
from jax import lax
from jax.experimental import pallas as pl
from jax.experimental.pallas import tpu as pltpu
from jax.sharding import PartitionSpec as P

F32 = jnp.float32
BF16 = jnp.bfloat16
NB = 256
SB = 64
TILE = 768
GROUP = 4
BLK = 512
KEYS = 16
HIGHEST = lax.Precision.HIGHEST
VMEM_LIMIT = 56 << 20


def mm(a, b, ca, cb):
    return lax.dot_general(
        a, b, (((ca,), (cb,)), ((), ())), precision=HIGHEST, preferred_element_type=F32
    )


def mm_bf(a, b, ca, cb):
    return lax.dot_general(a, b, (((ca,), (cb,)), ((), ())), preferred_element_type=F32)


def split2(x):
    hi = x.astype(BF16)
    return hi, (x - hi.astype(F32)).astype(BF16)


def mm3(a, b, ca, cb):
    return mm_bf(a[0], b[0], ca, cb) + (mm_bf(a[0], b[1], ca, cb) + mm_bf(a[1], b[0], ca, cb))


def split3(x):
    hi = x.astype(BF16)
    rest = x - hi.astype(F32)
    mid = rest.astype(BF16)
    low = (rest - mid.astype(F32)).astype(BF16)
    return hi, mid, low


def call(kernel, name, us, **kw):
    return pl.pallas_call(
        kernel,
        name=name,
        cost_estimate=pl.CostEstimate(flops=us * 10**9, transcendentals=0, bytes_accessed=1 << 20),
        compiler_params=pltpu.CompilerParams(vmem_limit_bytes=VMEM_LIMIT),
        **kw,
    )


def factor_small(diag):
    n = SB
    ri = lax.broadcasted_iota(jnp.int32, (n, n), 0)
    ci = lax.broadcasted_iota(jnp.int32, (n, n), 1)
    full = jnp.concatenate([diag, jnp.where(ri == ci, 1.0, 0.0)], axis=1)
    nv = n // 8
    rows = [full[8 * v : 8 * v + 8, :] for v in range(nv)]
    sub = lax.broadcasted_iota(jnp.int32, (8, 2 * n), 0)
    wide = lambda x: jnp.broadcast_to(x, (8, 2 * n))
    pivots = []
    for j0 in range(0, n, GROUP):
        v0 = j0 // 8
        cols = [[wide(rows[v][:, j0 + q : j0 + q + 1]) for v in range(v0, nv)] for q in range(GROUP)]
        at = [(j0 + q) % 8 for q in range(GROUP)]
        lead = [wide(rows[v0][at[q] : at[q] + 1, :]) for q in range(GROUP)]
        for q in range(GROUP):
            inv = 1.0 / wide(cols[q][0][at[q] : at[q] + 1, :])
            pivots.append(inv)
            scaled = lead[q] * inv
            below = [jnp.where(sub > at[q], cols[q][0], 0.0)] + cols[q][1:]
            for t in range(q + 1, GROUP):
                ratio = wide(cols[t][0][at[q] : at[q] + 1, :]) * inv
                weight = wide(cols[q][0][at[t] : at[t] + 1, :])
                cols[t] = [cols[t][i] - below[i] * ratio for i in range(len(below))]
                lead[t] = lead[t] - weight * scaled
            for i in range(len(below)):
                rows[v0 + i] = rows[v0 + i] - below[i] * scaled
    out = []
    for v in range(nv):
        scale = pivots[8 * v]
        for s in range(1, 8):
            scale = jnp.where(sub == s, pivots[8 * v + s], scale)
        out.append(rows[v] * jnp.sqrt(scale))
    return jnp.concatenate(out, axis=0)


def factor_diag(d_ref, w_ref, base):
    ri = lax.broadcasted_iota(jnp.int32, (NB, NB), 0)
    ci = lax.broadcasted_iota(jnp.int32, (NB, NB), 1)
    w_ref[...] = jnp.where(ri == ci, 1.0, 0.0)
    cb = lax.broadcasted_iota(jnp.int32, (SB, NB), 1)
    rb = lax.broadcasted_iota(jnp.int32, (SB, NB), 0)
    block = pl.ds(base, NB)
    for lo in range(0, NB, SB):
        hi = lo + SB
        here = pl.ds(base + lo, SB)
        strip = d_ref[here, block]
        small = factor_small(strip[:, lo:hi])
        both = mm(small[:, SB:], jnp.concatenate([strip, w_ref[lo:hi, :]], axis=1), 1, 0)
        up = jnp.where(cb >= rb + lo, both[:, :NB], 0.0)
        inv = jnp.where(cb <= rb + lo, both[:, NB:], 0.0)
        d_ref[here, block] = up
        w_ref[lo:hi, :] = inv
        if hi < NB:
            update = mm(up[:, hi:], jnp.concatenate([up, inv], axis=1), 0, 0)
            d_ref[pl.ds(base + hi, NB - hi), block] -= update[:, :NB]
            w_ref[hi:, :] -= update[:, NB:]


def factor_all(n, u_ref, w_ref):
    if n == NB:
        factor_diag(u_ref, w_ref.at[0], 0)
        return

    def step(p, carry):
        factor_diag(u_ref, w_ref.at[p], pl.multiple_of(p * NB, NB))
        for lo in range(0, n - NB, NB):

            @pl.when(p == lo // NB)
            def _():
                hi = lo + NB
                right = mm(w_ref[lo // NB], u_ref[lo:hi, hi:], 1, 0)
                u_ref[lo:hi, hi:] = right
                for q in range(hi, n, NB):
                    own = right[:, q - hi : q - hi + NB]
                    u_ref[q : q + NB, q:] -= mm(own, right[:, q - hi :], 0, 0)

        return carry

    lax.fori_loop(0, n // NB, step, 0)
    for lo in range(NB, n, NB):
        u_ref[lo : lo + NB, :lo] = jnp.zeros((NB, lo), F32)


def chol_kernel(n, a_ref, u_ref, w_ref):
    u_ref[...] = a_ref[...]
    factor_all(n, u_ref, w_ref)


def cholesky_upper(a, name):
    n = a.shape[0]
    return call(
        partial(chol_kernel, n),
        name,
        15,
        out_shape=(
            jax.ShapeDtypeStruct((n, n), F32),
            jax.ShapeDtypeStruct((n // NB, NB, NB), F32),
        ),
    )(a)


def one_hot(pos_row, n):
    ids = lax.broadcasted_iota(jnp.int32, (n, pos_row.shape[1]), 0)
    return jnp.where(ids == pos_row, 1.0, 0.0).astype(BF16)


CORNER = (((0, 0), (0, 1), (1, 1), (2, 0), (3, 0)), ((1, 2), (2, 2), (1, 3), (2, 3), (3, 3)))


def pack_kernel(at_ref, pos_ref, f_ref, o_ref):
    on_top = at_ref[0] == 0
    pivot_cols = at_ref[1] < 2
    inner = jnp.logical_not(jnp.logical_or(on_top, pivot_cols))

    for h in range(2):

        @pl.when(jnp.logical_and(on_top, at_ref[1] == h))
        def _():
            for y in range(4):
                for p in range(KEYS):
                    for t in range(5):
                        at = (p * 5 + t) * 8
                        rb, cb = CORNER[h][at // 128]
                        row = rb * NB + y * 64 + at % 64
                        lane = (cb - 2 * h) * NB + (at % 128) // 64 * 128
                        o_ref[y, 0, p, t * 8 : t * 8 + 8, :] = f_ref[
                            0, row : row + 8, lane : lane + 128
                        ]

    @pl.when(jnp.logical_and(on_top, jnp.logical_not(pivot_cols)))
    def _():
        place = one_hot(pos_ref[0, 2:3, :], BLK)
        out = sum(mm_bf(part, place, 1, 1) for part in split3(f_ref[0]))
        for y in range(4):
            for p in range(KEYS):
                o_ref[y, 0, p] = out[p * 64 : (p + 1) * 64, y * 128 : (y + 1) * 128]

    def store(b, total):
        for y in range(4):
            for p in range(KEYS):
                o_ref[y, 0, p, b * 32 : (b + 1) * 32, :] = total[
                    p * 32 : (p + 1) * 32, y * 128 : (y + 1) * 128
                ]

    def by_row(b):
        place_row = one_hot(pos_ref[0, b : b + 1, :], BLK)
        return [mm_bf(place_row, part, 1, 0) for part in split3(f_ref[0, b * BLK : (b + 1) * BLK, :])]

    @pl.when(jnp.logical_and(jnp.logical_not(on_top), pivot_cols))
    def _():
        for b in range(2):
            store(b, sum(by_row(b)))

    @pl.when(inner)
    def _():
        place_col = one_hot(pos_ref[0, 2:3, :], BLK)
        for b in range(2):
            store(b, sum(mm_bf(place_col, row.astype(BF16), 1, 1) for row in by_row(b)))


def chol_gathered_kernel(at_ref, a_ref, u_ref, w_ref):
    for yy in range(4):
        back = (at_ref[0] - yy) & 3
        for pc in range(KEYS):
            for t in range(5):
                at = (pc * 5 + t) * 8
                blk, q, i = at // 128, (at % 128) // 64, at % 64
                for h in range(2):
                    rb, cb = CORNER[h][blk]
                    row = rb * NB + yy * 64 + i
                    lane = cb * NB + q * 128
                    u_ref[row : row + 8, lane : lane + 128] = a_ref[pc, back, h, t * 8 : t * 8 + 8]
    for cb in (2, 3):
        u_ref[0:NB, cb * NB : (cb + 1) * NB] = u_ref[cb * NB : (cb + 1) * NB, 0:NB].T
    factor_all(u_ref.shape[0], u_ref, w_ref)


def pair(ref, rows, cols):
    return ref[0, rows, cols], ref[1, rows, cols]


def put(ref, rows, cols, value):
    ref[0, rows, cols], ref[1, rows, cols] = split2(value)


def rows_kernel(at_ref, u_ref, w_ref, x_ref, rxs_ref, o_ref, rx_ref, low_ref, inv_ref):
    step = pl.program_id(0)
    panels = u_ref.shape[0] // NB
    every = slice(None)
    strip = pl.ds(pl.multiple_of(at_ref[1] * 64, 64), 64)

    @pl.when(step == 0)
    def _():
        for p in range(panels):
            now, done = slice(p * NB, (p + 1) * NB), slice(0, p * NB)
            put(inv_ref, now, every, w_ref[p])
            if p:
                put(low_ref, now, done, u_ref[done, now].T)

    for p in range(panels):
        now, done = slice(p * NB, (p + 1) * NB), slice(0, p * NB)
        cur = jnp.concatenate([x_ref[4 * p : 4 * p + 4, t].reshape(NB, 128) for t in range(4)], axis=1)
        if p:
            cur = cur - mm3(pair(low_ref, now, done), pair(rxs_ref, done, every), 1, 0)
        cur = mm3(pair(inv_ref, now, every), split2(cur), 1, 0)
        rx_ref[now, :] = cur
        put(rxs_ref, now, every, cur)
    o_ref[1] = rx_ref[strip, NB:]

    @pl.when(step > 0)
    def _():
        o_ref[0] = rx_ref[strip, :NB]

    @pl.when(step == 0)
    def _():
        for yy in range(4):

            @pl.when(at_ref[0] == yy)
            def _():
                o_ref[0] = u_ref[strip, yy * NB : (yy + 1) * NB]


def halves(c0, c1):
    lane = lax.broadcasted_iota(jnp.int32, c0.shape, 1)
    first = jnp.where(lane < 64, c0, pltpu.roll(c1, 64, 1))
    return first, jnp.where(lane < 64, pltpu.roll(c0, 64, 1), c1)


def store_halves(core, mine_ref, other_ref, rows, c0, c1):
    first, second = halves(c0, c1)

    @pl.when(core == 0)
    def _():
        mine_ref[rows, :], other_ref[rows, :] = first, second

    @pl.when(core != 0)
    def _():
        mine_ref[rows, :], other_ref[rows, :] = second, first


def split_kernel(at_ref, c_ref, mine_ref, other_ref):
    c0 = c_ref[0, 2:, 0:32, :].reshape(448, 128)
    c1 = c_ref[0, 2:, 32:64, :].reshape(448, 128)
    store_halves(at_ref[2], mine_ref, other_ref, slice(None), c0, c1)


def schur_kernel(
    at_ref, u_ref, w_ref, y_ref, rp_ref, rxs_ref, c_ref, mine_ref, other_ref, t_ref, ry_ref
):
    step = pl.program_id(0)
    panels = u_ref.shape[0] // NB
    every, cols = slice(None), slice(NB, NB + 448)

    @pl.when(step == 0)
    def _():
        for h in range(2):
            ry_ref[h, :NB, :] = rp_ref[h].astype(F32).T.astype(BF16)
        for p in range(panels):
            now, done = slice(p * NB, (p + 1) * NB), slice(0, p * NB)
            cur = jnp.concatenate(
                [
                    y_ref[(at_ref[0] - (2 * p + t)) & 3, :, (2 * p + t) // 4].reshape(448, 128)
                    for t in range(2)
                ],
                axis=1,
            )
            if p:
                cur = cur - mm3(pair(ry_ref, cols, done), split2(u_ref[done, now]), 1, 0)
            put(ry_ref, cols, now, mm3(split2(cur), split2(w_ref[p]), 1, 1))
        t_ref[:, NB + 448 :] = jnp.zeros((NB, 64), F32)
        t_ref[:, : NB + 448] = -mm3(pair(ry_ref, slice(0, NB), every), pair(ry_ref, every, every), 1, 1)

    @pl.when(step > 0)
    def _():
        prod = -mm3(pair(ry_ref, every, every), pair(rxs_ref, every, every), 1, 0)
        store_halves(
            at_ref[2], mine_ref, other_ref, slice(0, NB), prod[:NB, :128], prod[:NB, 128:]
        )
        c0 = c_ref[0, 2:, 0:32, :].reshape(448, 128) + prod[cols, :128]
        c1 = c_ref[0, 2:, 32:64, :].reshape(448, 128) + prod[cols, 128:]
        store_halves(at_ref[2], mine_ref, other_ref, cols, c0, c1)


def unpack_kernel(row_ref, pos_ref, r_ref, o_ref):
    for k in range(2):

        @pl.when(row_ref[0] == 0)
        def _():
            for yy in range(4):
                o_ref[k, :, yy * NB : (yy + 1) * NB] = r_ref[2 * yy + k]

        @pl.when(row_ref[0] != 0)
        def _():
            for b in range(2):
                here = slice(b * 128, (b + 1) * 128)
                wide = jnp.concatenate([r_ref[2 * yy + k, :, here] for yy in range(4)], axis=1)
                place = one_hot(pos_ref[k, b : b + 1, :], BLK)
                o_ref[k, :, b * BLK : (b + 1) * BLK] = sum(
                    mm_bf(part, place, 1, 0) for part in split3(wide)
                )


def load_parts(core_ref, s_ref, g_ref, part_ref):
    core = core_ref[0]
    part_ref[core, 0], part_ref[core, 1] = split2(s_ref[...])
    part_ref[1 - core, 0], part_ref[1 - core, 1] = split2(g_ref[...])


def merge_kernel(core_ref, tx_ref, ty_ref, s_ref, g_ref, p_ref, o_ref, part_ref, ey_ref):
    tile = pl.program_id(0)

    @pl.when(tile == 0)
    def _():
        for k in range(2):
            ey_ref[k] = one_hot(ty_ref[k], ey_ref.shape[1])
        load_parts(core_ref, s_ref, g_ref, part_ref)

    acc = p_ref[...]
    for k in range(2):
        ex = one_hot(tx_ref[k] - tile * NB, NB)
        for i in range(2):
            half = mm_bf(ex, part_ref[k, i], 1, 1)
            acc = acc + mm_bf(half.astype(BF16), ey_ref[k], 1, 1)
    o_ref[...] = acc


def side_kernel(core_ref, tx_ref, ty_ref, s_ref, g_ref, p_ref, o_ref, part_ref):
    tile = pl.program_id(0)

    @pl.when(tile == 0)
    def _():
        core = core_ref[0]
        for ref, k in ((s_ref, core), (g_ref, 1 - core)):
            ey = one_hot(ty_ref[k], NB)
            for i, part in enumerate(split2(ref[...])):
                part_ref[k, i] = mm_bf(ey, part, 1, 0).astype(BF16)

    acc = p_ref[...]
    for k in range(2):
        ex = one_hot(tx_ref[k] - tile * TILE, TILE)
        for i in range(2):
            acc = acc + mm_bf(ex, part_ref[k, i], 1, 1)
    o_ref[...] = acc


def final_kernel(
    core_ref, tx_ref, ty_ref, s_ref, g_ref, t_ref, tg_ref, w_ref, p_ref, row_ref, col_ref,
    o_ref, f_ref, part_ref, ey_ref, rc_ref, rt_ref,
):
    tile = pl.program_id(0)
    inv = split2(w_ref[0])

    @pl.when(tile == 0)
    def _():
        for k in range(2):
            ey_ref[k] = one_hot(ty_ref[k], 768)
        load_parts(core_ref, s_ref, g_ref, part_ref)
        top = col_ref[...]
        core = core_ref[0]
        for ref, k in ((t_ref, core), (tg_ref, 1 - core)):
            for part in split2(ref[:, NB : NB + 448]):
                top = top + mm_bf(part, ey_ref[k], 1, 1)
        rc_ref[0], rc_ref[1] = split2(mm3(inv, split2(top), 1, 0))

    acc = p_ref[...]
    left = row_ref[...]
    for k in range(2):
        ex = one_hot(tx_ref[k] - tile * TILE, TILE)
        for i in range(2):
            half = mm_bf(ex, part_ref[k, i], 1, 1)
            left = left + half[:, :NB]
            acc = acc + mm_bf(half[:, NB:].astype(BF16), ey_ref[k], 1, 1)
    rows = mm3(split2(left), inv, 1, 1)
    rt_ref[...] = rows.T
    f_ref[...] = rt_ref[pl.ds(pl.multiple_of(core_ref[2] * 16, 16), 16), :]
    out = acc - mm3(split2(rows), (rc_ref[0], rc_ref[1]), 1, 0)
    lane = lax.broadcasted_iota(jnp.int32, out.shape, 1)
    row = tile * TILE + lax.broadcasted_iota(jnp.int32, out.shape, 0)
    keep_row = jnp.logical_or(core_ref[1] != 0, row >= NB)
    keep = jnp.logical_and(keep_row, jnp.logical_or(core_ref[2] != 0, lane >= NB))
    o_ref[...] = jnp.where(keep, out, 0.0)


def call_core(kernel, name, us, grid, in_specs, out_specs, scratch_shapes, out_shape):
    return pl.pallas_call(
        kernel,
        name=name,
        cost_estimate=pl.CostEstimate(flops=us * 10**9, transcendentals=0, bytes_accessed=1 << 20),
        compiler_params=pltpu.CompilerParams(vmem_limit_bytes=VMEM_LIMIT),
        grid_spec=pltpu.PrefetchScalarGridSpec(
            num_scalar_prefetch=1,
            grid=grid,
            in_specs=in_specs,
            out_specs=out_specs,
            scratch_shapes=scratch_shapes,
        ),
        out_shape=out_shape,
    )


def smem():
    return pl.BlockSpec(memory_space=pltpu.SMEM)


def whole(shape):
    return pl.BlockSpec(shape, lambda *_: (0,) * len(shape))


def local(child_fronts, parent_front, child_map):
    r = lax.axis_index("row")
    c = lax.axis_index("col")
    core = r % 2
    y = r // 2
    nblk = child_map.shape[1] // BLK

    maps = child_map.reshape(2 * nblk, BLK)
    keys = maps // 768
    hot = (keys[:, :, None] == jnp.arange(KEYS, dtype=jnp.int32)).astype(BF16)
    lower = (jnp.arange(BLK)[:, None] >= jnp.arange(BLK)[None, :]).astype(BF16)
    counts = jnp.einsum("ef,bfk->bek", lower, hot, preferred_element_type=F32)
    rank = jnp.sum(counts * hot.astype(F32), axis=2).astype(jnp.int32) - 1
    pos = (keys * 32 + rank).reshape(2, nblk, BLK)
    maps = maps.reshape(2, nblk, BLK)

    pos_own = lax.dynamic_index_in_dim(pos, core, 0, keepdims=False)
    maps_own = lax.dynamic_index_in_dim(maps, core, 0, keepdims=False)
    pos_c = lax.dynamic_slice_in_dim(pos, jnp.maximum(c - 2, 0), 1, axis=1)
    pos_r = lax.dynamic_slice_in_dim(pos, jnp.maximum(2 * r - 2, 0), 2, axis=1)

    def sorted_maps(start, count):
        ids = start + jnp.arange(count, dtype=jnp.int32)
        return jnp.sum(
            jnp.where(pos[:, :, :, None] == ids, maps[:, :, :, None], 0), axis=2, dtype=jnp.int32
        )

    to_rows = sorted_maps(r * 64, 64).reshape(2, 1, 896) - r * 1536
    to_cols = sorted_maps(c * 32, 32).reshape(2, 1, 448) - c * 768
    shifts = [[(i, (i + 2 * s) % 8) for i in range(8)] for s in (1, 2, 3)]

    def gather_y(x):
        return jnp.stack([x] + [lax.ppermute(x, "row", pairs) for pairs in shifts])

    def swap(x, axes):
        return lax.all_to_all(x, axes, split_axis=0, concat_axis=0, tiled=True)

    def repeat(x, axes, parts):
        x = lax.optimization_barrier(x)
        return swap(jnp.broadcast_to(x[None], (parts, *x.shape)), axes)

    at = jnp.stack([y, c, core])
    packed = call(
        pack_kernel,
        "pack",
        8,
        grid=(2,),
        in_specs=[
            smem(),
            pl.BlockSpec((1, 3, BLK), lambda k: (k, 0, 0)),
            pl.BlockSpec((1, 1024, BLK), lambda k: (k, 0, 0)),
        ],
        out_specs=pl.BlockSpec((4, 1, KEYS, 64, 128), lambda k: (0, k, 0, 0, 0)),
        out_shape=jax.ShapeDtypeStruct((4, 2, KEYS, 64, 128), F32),
    )(jnp.stack([r, c]), jnp.concatenate([pos_r, pos_c], axis=1), child_fronts)
    arrived = swap(packed.reshape(8 * KEYS, 64, 128), ("row", "col")).reshape(8, KEYS, 64, 128)
    spread = gather_y(arrived[0, :2, :40])
    pieces = lax.all_gather(spread, "col")

    pivot_ids = jnp.sum(
        jnp.where(
            pos_own[:, :, None] == jnp.arange(32, dtype=jnp.int32), maps_own[:, :, None], 0
        ),
        axis=1,
        dtype=jnp.int32,
    )
    pick = (pivot_ids[:, :, None] == jnp.arange(NB, dtype=jnp.int32)).astype(F32)
    pivot_x = jnp.einsum("bis,bsp->ip", arrived[0, 2:, :, :32], pick, precision=HIGHEST)
    moved = pivot_x
    for s, pairs in enumerate(shifts):
        got = lax.ppermute(pivot_x, "row", pairs)
        moved = jnp.where(y == s + 1, got, moved)
    moved = jnp.stack([moved[:, :128], moved[:, 128:]])
    own_x, _ = lax.optimization_barrier((jnp.concatenate([moved, arrived[0, 2:]]), spread))
    panel_x = lax.all_gather(own_x, "col")

    raw, raw_other = call(
        split_kernel,
        "split",
        4,
        grid=(7,),
        in_specs=[smem(), pl.BlockSpec((1, KEYS, 64, 128), lambda g: (g + 1, 0, 0, 0))],
        out_specs=[pl.BlockSpec((448, 128), lambda g: (0, g))] * 2,
        out_shape=[jax.ShapeDtypeStruct((448, 896), F32)] * 2,
    )(at, arrived)
    sibling = [(i, i ^ 1) for i in range(8)]
    flags = jnp.stack([core, r, c])
    raw_got = lax.ppermute(raw_other, "row", sibling)

    def merge(kernel, name, us, rows, cols, tile, scratch):
        return call_core(
            kernel,
            name,
            us,
            (rows // tile,),
            [
                whole((2, 1, 896)),
                whole((2, 1, 448)),
                whole((448, 896)),
                whole((448, 896)),
                pl.BlockSpec((tile, cols), lambda t, which: (t, 0)),
            ],
            pl.BlockSpec((tile, cols), lambda t, which: (t, 0)),
            scratch,
            jax.ShapeDtypeStruct((rows, cols), F32),
        )(flags, to_rows, to_cols, raw, raw_got, parent_front)

    top = merge(
        merge_kernel,
        "merge_top",
        7,
        NB,
        768,
        NB,
        [pltpu.VMEM((2, 2, 448, 896), BF16), pltpu.VMEM((2, 768, 448), BF16)],
    )
    side = merge(side_kernel, "merge_side", 8, 1536, NB, TILE, [pltpu.VMEM((2, 2, NB, 896), BF16)])
    top = swap(top.reshape(8, 32, 768), "row")[0]
    pieces, top, side = lax.optimization_barrier((pieces, top, side))
    top = repeat(top, "row", 8).reshape(NB, 768)
    upper, inverses = call(
        chol_gathered_kernel,
        "child_factor",
        64,
        in_specs=[smem(), whole((KEYS, 4, 2, 40, 128))],
        out_shape=(
            jax.ShapeDtypeStruct((1024, 1024), F32),
            jax.ShapeDtypeStruct((4, NB, NB), F32),
        ),
    )(at, pieces)
    panel_x, upper, top, mine_y = lax.optimization_barrier((panel_x, upper, top, arrived[1:, :2]))
    shifted_y = [lax.ppermute(mine_y, "row", pairs) for pairs in shifts]
    side = swap(jnp.concatenate([side, top[:, :NB]]).reshape(KEYS, 112, NB), "col")[0]
    factor_x, outgoing = call(
        rows_kernel,
        "rows",
        24,
        grid=(4,),
        in_specs=[
            smem(),
            whole((1024, 1024)),
            whole((4, NB, NB)),
            pl.BlockSpec((KEYS, 4, 64, 128), lambda g: (0, g, 0, 0)),
        ],
        out_specs=(
            pl.BlockSpec((2, 1024, BLK), lambda g: (0, 0, g)),
            pl.BlockSpec((2, 64, NB), lambda g: (g, 0, 0)),
        ),
        out_shape=(
            jax.ShapeDtypeStruct((2, 1024, 2048), BF16),
            jax.ShapeDtypeStruct((8, 64, NB), F32),
        ),
        scratch_shapes=[
            pltpu.VMEM((1024, BLK), F32),
            pltpu.VMEM((2, 1024, 1024), BF16),
            pltpu.VMEM((2, 1024, NB), BF16),
        ],
    )(at, upper, inverses, panel_x)
    factor_x, side = lax.optimization_barrier((factor_x, side))
    left = repeat(side, "col", KEYS).reshape(1792, NB)
    panel_y = jnp.stack([mine_y, *shifted_y])
    schur, other, cross = call(
        schur_kernel,
        "schur",
        25,
        grid=(8,),
        in_specs=[
            smem(),
            whole((1024, 1024)),
            whole((4, NB, NB)),
            whole((4, 7, 2, 64, 128)),
            pl.BlockSpec((2, 1024, NB), lambda g: (0, 0, 0)),
            pl.BlockSpec((2, 1024, NB), lambda g: (0, 0, jnp.maximum(g, 1))),
            pl.BlockSpec((1, KEYS, 64, 128), lambda g: (jnp.maximum(g, 1), 0, 0, 0)),
        ],
        out_specs=(
            pl.BlockSpec((NB + 448, 128), lambda g: (0, jnp.maximum(g, 1) - 1)),
            pl.BlockSpec((NB + 448, 128), lambda g: (0, jnp.maximum(g, 1) - 1)),
            whole((NB, 768)),
        ),
        out_shape=(
            jax.ShapeDtypeStruct((NB + 448, 896), F32),
            jax.ShapeDtypeStruct((NB + 448, 896), F32),
            jax.ShapeDtypeStruct((NB, 768), F32),
        ),
        scratch_shapes=[pltpu.VMEM((2, NB + 448, 1024), BF16)],
    )(at, upper, inverses, panel_y, factor_x, factor_x, arrived)

    cross_got = lax.ppermute(cross, "row", sibling)
    got = lax.ppermute(other, "row", sibling)
    left, outgoing = lax.optimization_barrier((left, outgoing))
    landed = swap(outgoing, "row")

    child_factor = call(
        unpack_kernel,
        "unpack",
        4,
        in_specs=[smem(), whole((2, 2, BLK)), whole((8, 64, NB))],
        out_shape=jax.ShapeDtypeStruct((2, 64, 1024), F32),
    )(r[None], pos_r, landed).swapaxes(1, 2)

    corner = left[1536:] + cross[:, :NB] + cross_got[:, :NB]
    _, parent_inverse = cholesky_upper(corner, "parent_factor")
    schur_out, rows_out = call_core(
        final_kernel,
        "final",
        32,
        (1536 // TILE,),
        [
            whole((2, 1, 896)),
            whole((2, 1, 448)),
            whole((NB + 448, 896)),
            whole((NB + 448, 896)),
            whole((NB, 768)),
            whole((NB, 768)),
            whole((1, NB, NB)),
            pl.BlockSpec((TILE, 768), lambda t, which: (t, 0)),
            pl.BlockSpec((TILE, NB), lambda t, which: (t, 0)),
            whole((NB, 768)),
        ],
        (
            pl.BlockSpec((TILE, 768), lambda t, which: (t, 0)),
            pl.BlockSpec((16, TILE), lambda t, which: (0, t)),
        ),
        [
            pltpu.VMEM((2, 2, NB + 448, 896), BF16),
            pltpu.VMEM((2, 768, 448), BF16),
            pltpu.VMEM((2, NB, 768), BF16),
            pltpu.VMEM((NB, TILE), F32),
        ],
        (
            jax.ShapeDtypeStruct((1536, 768), F32),
            jax.ShapeDtypeStruct((16, 1536), F32),
        ),
    )(flags, to_rows, to_cols, schur, got, cross, cross_got, parent_inverse, parent_front, left, top)
    return child_factor, rows_out.T, schur_out


def solution(mesh):
    return jax.shard_map(
        local,
        mesh=mesh,
        in_specs=(P(None, "row", "col"), P("row", "col"), P()),
        out_specs=(P(None, "row", "col"), P("row", "col"), P("row", "col")),
        check_vma=False,
    )
```
